128 devices in a mesh: shard: 16 (over y, x), tensor: 8 (over z, core).
Axes of the slice: x: 4, y: 4, z: 4, core: 2. Of those that a mesh axis runs over, the one named last changes fastest.
Arguments:
- gradients: bfloat16 [4, 512, 6144], P(None, ('shard', 'tensor')), may hold values from -6 to 6
- adam_mean: float32 [4, 512, 6144], P(None, ('shard', 'tensor')), may hold values from -14 to 14
- adam_square: float32 [4, 512, 6144], P(None, ('shard', 'tensor')), may hold values from 0.001 to 0.05
- stat_left: float32 [128, 3, 512, 512], P(('shard', 'tensor')), may hold values from -2 to 30, as said below
- stat_right: float32 [128, 3, 128, 128], P(('shard', 'tensor')), may hold values from -12 to 120, as said below
- root_left: float32 [128, 3, 512, 512], P(('shard', 'tensor')), may hold values from -0.1 to 0.6, as said below
- root_right: float32 [128, 3, 128, 128], P(('shard', 'tensor')), may hold values from -0.1 to 0.4, as said below
- owners: int32 [192], replicated, may hold values from 0 to 127, as said below
- small_grad: float32 [6336], replicated, may hold values from -1.2 to 1.2
- small_mean: float32 [6336], replicated, may hold values from -0.6 to 0.6
- small_square: float32 [6336], replicated, may hold values from 0.001 to 0.05
Outputs:
- updates: float32 [4, 512, 6144], P(None, ('shard', 'tensor'))
- mean_out: float32 [4, 512, 6144], P(None, ('shard', 'tensor'))
- square_out: float32 [4, 512, 6144], P(None, ('shard', 'tensor'))
- left_out: float32 [128, 3, 512, 512], P(('shard', 'tensor'))
- right_out: float32 [128, 3, 128, 128], P(('shard', 'tensor'))
- small_update: float32 [6336], replicated
- small_mean_out: float32 [6336], replicated
- small_square_out: float32 [6336], replicated
The draws below stay inside these ranges and needn't reach their ends.
Inputs may be any that keep to these rules, and one draw needn't show every extreme that they name: `owners`: no device owns more than 3 blocks, and some device owns exactly 3. `stat_left`: symmetric. `stat_right`: symmetric. `root_left`: symmetric. `root_right`: symmetric.
All inputs are finite; a program needn't handle non-finite values.
Results may differ from the reference program's by a relative error of at most 0.00095.
Values may be sent and summed in bfloat16 or wider, within the bound.
A program may use at most 64 MiB of HBM per device.

```python
import math
import jax
import jax.numpy as jnp
from jax import lax

D = 512
BLOCK = 128
LAYERS = 4
COLS = 6144
BLOCKS = 192
CAP = 3
SMALL = 6336
DEVICES = 128


def log_spread(key, length, low, high):
    return jnp.exp(jax.random.uniform(key, (length,), jnp.float32, math.log(low), math.log(high)))


def symmetric(base, diag, spread, size):
    ident = (jnp.arange(size)[:, None] == jnp.arange(size)[None, :]).astype(jnp.float32)
    mixed = (base + jnp.swapaxes(base, 2, 3)) * (spread / math.sqrt(2.0))
    return mixed * (1.0 - ident) + diag * ident


def draw_gradients(key, part):
    first, second, third = jax.random.split(key, 3)
    row_scale = log_spread(first, D, 0.3, 3.0)
    col_scale = log_spread(second, COLS, 0.3, 3.0)
    values = 0.1 * jax.random.truncated_normal(third, -4.0, 4.0, (LAYERS, D, COLS), jnp.float32)
    return (values * row_scale[None, :, None] * col_scale[None, None, :]).astype(jnp.bfloat16)


def draw_adam_mean(key, part):
    first, second, third = jax.random.split(key, 3)
    rising = 3.0 ** (jnp.arange(D).astype(jnp.float32) / (D - 1))
    row_scale = log_spread(first, D, 0.3, 3.0) * rising
    col_scale = log_spread(second, COLS, 0.3, 3.0)
    values = 0.1 * jax.random.truncated_normal(third, -4.0, 4.0, (LAYERS, D, COLS), jnp.float32)
    return values * row_scale[None, :, None] * col_scale[None, None, :]


def draw_stat_left(key, part):
    first, second = jax.random.split(key)
    shape = (DEVICES, CAP, D, D)
    base = jax.random.truncated_normal(first, -4.0, 4.0, shape, jnp.float32)
    diag = jax.random.uniform(second, (DEVICES, CAP, D, 1), jnp.float32, 15.0, 30.0)
    return symmetric(base, diag, 0.3, D)


def draw_stat_right(key, part):
    first, second = jax.random.split(key)
    shape = (DEVICES, CAP, BLOCK, BLOCK)
    base = jax.random.truncated_normal(first, -4.0, 4.0, shape, jnp.float32)
    diag = jax.random.uniform(second, (DEVICES, CAP, BLOCK, 1), jnp.float32, 60.0, 120.0)
    return symmetric(base, diag, 2.0, BLOCK)


def draw_root_left(key, part):
    first, second = jax.random.split(key)
    shape = (DEVICES, CAP, D, D)
    base = jax.random.truncated_normal(first, -4.0, 4.0, shape, jnp.float32)
    diag = jax.random.uniform(second, (DEVICES, CAP, D, 1), jnp.float32, 0.4, 0.6)
    return symmetric(base, diag, 0.12 / math.sqrt(D), D)


def draw_root_right(key, part):
    first, second = jax.random.split(key)
    shape = (DEVICES, CAP, BLOCK, BLOCK)
    base = jax.random.truncated_normal(first, -4.0, 4.0, shape, jnp.float32)
    diag = jax.random.uniform(second, (DEVICES, CAP, BLOCK, 1), jnp.float32, 0.25, 0.4)
    return symmetric(base, diag, 0.08 / math.sqrt(BLOCK), BLOCK)


def draw_owners(key, part):
    first, second, third, fourth = jax.random.split(key, 4)
    total = DEVICES * CAP
    places = jnp.arange(total, dtype=jnp.int32)
    device_of = places // CAP
    full_device = jax.random.randint(first, (), 0, DEVICES)
    weights = jax.random.randint(second, (DEVICES,), 0, 4)
    noise = jax.random.randint(third, (total,), 0, 1024)
    scores = jnp.where(device_of == full_device, 1 << 20, weights[device_of] * 256 + noise)
    scores = scores * total + places
    picked_scores, chosen = lax.top_k(scores, BLOCKS)
    chosen_owners = device_of[chosen]
    shuffle = jax.random.permutation(fourth, BLOCKS)
    return chosen_owners[shuffle].astype(jnp.int32)


def steps_of(key, shape, shards, least, top_value):
    gain = 1.0
    for axis_at, shards_of in shards:
        heights = jax.random.uniform(jax.random.fold_in(jax.random.fold_in(key, 6), axis_at), (shards_of,), jnp.float32, least / len(shards), top_value / len(shards))
        gain = gain * jnp.repeat(jnp.exp(heights), shape[axis_at] // shards_of).reshape((-1,) + (1,) * (len(shape) - 1 - axis_at))
    return gain


def normal_values(stream_key, shape, width, bound, held_as=jnp.bfloat16):
    return jnp.clip(width * jax.random.normal(stream_key, shape, jnp.float32), -bound, bound).astype(held_as)


def setup_inputs(seed: int = 0) -> dict:
    seeds = jax.random.split(jax.random.key(seed), 12)
    return {
        "gradients": draw_gradients(jax.random.fold_in(seeds[11], 71), 0),
        "adam_mean": draw_adam_mean(jax.random.fold_in(seeds[11], 71), 0),
        "adam_square": jnp.clip(jnp.exp(math.log(0.05) - 3.912023 * jax.random.uniform(seeds[2], (LAYERS, D, COLS), jnp.float32) ** steps_of(seeds[2], (LAYERS, D, COLS), ((1, 128),), -0.2, 0.2)), 0.001, 0.05),
        "stat_left": draw_stat_left(jax.random.fold_in(seeds[11], 71), 0),
        "stat_right": draw_stat_right(jax.random.fold_in(seeds[11], 71), 0),
        "root_left": draw_root_left(jax.random.fold_in(seeds[11], 71), 0),
        "root_right": draw_root_right(jax.random.fold_in(seeds[11], 71), 0),
        "owners": draw_owners(jax.random.fold_in(seeds[11], 71), 0),
        "small_grad": normal_values(seeds[8], (SMALL,), 0.2, 1.2, jnp.float32),
        "small_mean": normal_values(seeds[9], (SMALL,), 0.1, 0.6, jnp.float32),
        "small_square": jnp.clip(jnp.exp(jax.random.uniform(seeds[10], (SMALL,), jnp.float32, math.log(0.001), math.log(0.05))), 0.001, 0.05),
    }


PRECISE = lax.Precision.HIGHEST

def adam_moments(grad_wide, mean_old, square_old):
    mean_new = 0.9 * mean_old + 0.1 * grad_wide
    square_new = 0.95 * square_old + 0.05 * grad_wide * grad_wide
    return (mean_new, square_new, mean_new / (jnp.sqrt(square_new) + 1e-08))

def reference(gradients, adam_mean, adam_square, stat_left, stat_right, root_left, root_right, owners, small_grad, small_mean, small_square):
    layer_count, row_count, col_count = gradients.shape
    block_count = col_count // BLOCK
    total_blocks = layer_count * block_count
    grad_blocks = gradients.reshape(layer_count, row_count, block_count, BLOCK).transpose(0, 2, 1, 3).reshape(total_blocks, row_count, BLOCK)
    positions = jnp.arange(total_blocks, dtype=jnp.int32)
    earlier = (owners[:, None] == owners[None, :]) & (positions[None, :] < positions[:, None])
    slot_index = lax.optimization_barrier(jnp.sum(earlier.astype(jnp.int32), axis=1)).astype(jnp.int32)

    def one_block(packed):
        grad_block, device, slot_place = packed
        left_root = root_left[device, slot_place]
        right_root = root_right[device, slot_place]
        left_term = jnp.dot(grad_block, grad_block.T, preferred_element_type=jnp.float32)
        right_term = jnp.dot(grad_block.T, grad_block, preferred_element_type=jnp.float32)
        left_applied = jnp.dot(left_root, grad_block.astype(jnp.float32), precision=PRECISE)
        return (left_term, right_term, jnp.dot(left_applied, right_root, precision=PRECISE))
    left_terms, right_terms, precond = lax.map(one_block, (grad_blocks, owners, slot_index))
    left_out = stat_left.at[owners, slot_index].add(left_terms)
    right_out = stat_right.at[owners, slot_index].add(right_terms)
    grad_wide = gradients.astype(jnp.float32)
    mean_out, square_out, direction = adam_moments(grad_wide, adam_mean, adam_square)
    adam_sums = lax.optimization_barrier(jnp.sum(jnp.square(direction).reshape(layer_count, row_count, block_count, BLOCK), axis=(1, 3))).reshape(total_blocks)
    precond_sums = lax.optimization_barrier(jnp.sum(jnp.square(precond), axis=(1, 2)))
    graft_ratio = jnp.sqrt(adam_sums / (precond_sums + 1e-06))
    scaled = precond * graft_ratio[:, None, None]
    updates = scaled.reshape(layer_count, block_count, row_count, BLOCK).transpose(0, 2, 1, 3).reshape(layer_count, row_count, col_count)
    small_mean_out, small_square_out, small_update = adam_moments(small_grad, small_mean, small_square)
    return (updates, mean_out, square_out, left_out, right_out, small_update, small_mean_out, small_square_out)
```

```python
import jax
import jax.numpy as jnp
from jax import lax
from jax.sharding import PartitionSpec as P

BLOCK = 128


PRECISE = lax.Precision.HIGHEST


def adam_moments(grad_wide, mean_old, square_old):
    mean_new = 0.9 * mean_old + 0.1 * grad_wide
    square_new = 0.95 * square_old + 0.05 * grad_wide * grad_wide
    return (mean_new, square_new, mean_new / (jnp.sqrt(square_new) + 1e-08))


def per_device(
    gradients,
    adam_mean,
    adam_square,
    stat_left,
    stat_right,
    root_left,
    root_right,
    owners,
    small_grad,
    small_mean,
    small_square,
):
    layer_count, row_count, col_count = gradients.shape
    block_count = col_count // BLOCK
    devices = lax.axis_size(("shard", "tensor"))
    slot_count = stat_left.shape[1]
    total_blocks = owners.shape[0]
    positions = jnp.arange(total_blocks, dtype=jnp.int32)
    earlier = (owners[:, None] == owners[None, :]) & (positions[None, :] < positions[:, None])
    slot_index = jnp.sum(earlier.astype(jnp.int32), axis=1)
    target = slot_index * devices + owners
    places = jnp.arange(slot_count * devices, dtype=jnp.int32)
    picker = (
        (places[:, None] == target[None, :])
        .astype(jnp.bfloat16)
        .reshape(slot_count * devices, layer_count, block_count)
    )
    grad_wide = gradients.astype(jnp.float32)
    mean_out, square_out, direction = adam_moments(grad_wide, adam_mean, adam_square)
    adam_part = jnp.sum(
        jnp.square(direction).reshape(layer_count, row_count, block_count, BLOCK), axis=(1, 3)
    )
    part_by_place = jnp.zeros((slot_count * devices,), jnp.float32).at[target].set(
        adam_part.reshape(total_blocks)
    )
    part_hi = part_by_place.astype(jnp.bfloat16)
    part_lo = (part_by_place - part_hi.astype(jnp.float32)).astype(jnp.bfloat16)
    lane = jnp.arange(BLOCK, dtype=jnp.int32)
    extra = jnp.where(
        lane[None, :] == 0,
        part_hi[:, None],
        jnp.where(lane[None, :] == 1, part_lo[:, None], jnp.zeros((), jnp.bfloat16)),
    )[:, None, :]
    pieces = gradients.reshape(layer_count, row_count, block_count, BLOCK)
    outgoing = jnp.einsum(
        "qln,lrnb->qrb", picker, pieces, preferred_element_type=jnp.float32
    ).astype(jnp.bfloat16)
    outgoing = jnp.concatenate([outgoing, extra], axis=1)
    outgoing = outgoing.reshape(slot_count, devices, row_count + 1, BLOCK)
    incoming = lax.all_to_all(
        outgoing, ("shard", "tensor"), split_axis=1, concat_axis=1, tiled=True
    )
    block_grads = incoming[:, :, :row_count, :].reshape(slot_count, devices * row_count, BLOCK)
    adam_sums = jnp.sum(
        incoming[:, :, row_count, 0].astype(jnp.float32)
        + incoming[:, :, row_count, 1].astype(jnp.float32),
        axis=1,
    )
    left_out = (
        stat_left
        + jnp.einsum("cib,cjb->cij", block_grads, block_grads, preferred_element_type=jnp.float32)[
            None
        ]
    )
    right_out = (
        stat_right
        + jnp.einsum("cib,cid->cbd", block_grads, block_grads, preferred_element_type=jnp.float32)[
            None
        ]
    )
    left_applied = jnp.einsum(
        "cij,cjb->cib", root_left[0], block_grads.astype(jnp.float32), precision=PRECISE
    )
    precond = jnp.einsum("cib,cbd->cid", left_applied, root_right[0], precision=PRECISE)
    precond_sums = jnp.sum(jnp.square(precond), axis=(1, 2))
    graft_ratio = jnp.sqrt(adam_sums / (precond_sums + 1e-06))
    scaled = precond * graft_ratio[:, None, None]
    shaped = scaled.reshape(slot_count, devices, row_count, BLOCK)
    returned = lax.all_to_all(shaped, ("shard", "tensor"), split_axis=1, concat_axis=1, tiled=True)
    returned = returned.reshape(slot_count * devices, row_count, BLOCK)
    own_rows = jnp.take(returned, target, axis=0).reshape(
        layer_count, block_count, row_count, BLOCK
    )
    updates = own_rows.transpose(0, 2, 1, 3).reshape(layer_count, row_count, col_count)
    small_mean_out, small_square_out, small_update = adam_moments(
        small_grad, small_mean, small_square
    )
    return (
        updates,
        mean_out,
        square_out,
        left_out,
        right_out,
        small_update,
        small_mean_out,
        small_square_out,
    )


def solution(mesh):
    in_specs = (
        P(None, ("shard", "tensor"), None),
        P(None, ("shard", "tensor"), None),
        P(None, ("shard", "tensor"), None),
        P(("shard", "tensor"), None, None, None),
        P(("shard", "tensor"), None, None, None),
        P(("shard", "tensor"), None, None, None),
        P(("shard", "tensor"), None, None, None),
        P(),
        P(),
        P(),
        P(),
    )
    out_specs = (
        P(None, ("shard", "tensor"), None),
        P(None, ("shard", "tensor"), None),
        P(None, ("shard", "tensor"), None),
        P(("shard", "tensor"), None, None, None),
        P(("shard", "tensor"), None, None, None),
        P(),
        P(),
        P(),
    )
    return jax.shard_map(
        per_device, mesh=mesh, in_specs=in_specs, out_specs=out_specs, check_vma=False
    )
```

```python
import functools

import jax
import jax.numpy as jnp
from jax import lax
from jax.experimental import pallas as pl
from jax.experimental.pallas import tpu as pltpu
from jax.sharding import PartitionSpec as P

BLOCK = 128
MESH = pl.DeviceIdType.MESH


PRECISE = lax.Precision.HIGHEST


def adam_moments(grad_wide, mean_old, square_old):
    mean_new = 0.9 * mean_old + 0.1 * grad_wide
    square_new = 0.95 * square_old + 0.05 * grad_wide * grad_wide
    return (mean_new, square_new, mean_new / (jnp.sqrt(square_new) + 1e-08))


def _a2a_kernel(n, width, x_ref, y_ref, send_sem, recv_sem):
    me = lax.axis_index("shard") * width + lax.axis_index("tensor")

    def where(d):
        return (lax.div(d, width), lax.rem(d, width))

    barrier = pltpu.get_barrier_semaphore()

    def greet(j, c):
        pl.semaphore_signal(
            barrier, inc=1, device_id=where(lax.rem(me + j, n)), device_id_type=MESH
        )
        return c

    lax.fori_loop(1, n, greet, 0)
    pl.semaphore_wait(barrier, n - 1)

    def send(j, c):
        d = lax.rem(me + j, n)
        pltpu.make_async_remote_copy(
            src_ref=x_ref.at[pl.ds(d, 1)],
            dst_ref=y_ref.at[pl.ds(me, 1)],
            send_sem=send_sem,
            recv_sem=recv_sem,
            device_id=where(d),
            device_id_type=MESH,
        ).start()
        return c

    lax.fori_loop(1, n, send, 0)
    y_ref[pl.ds(me, 1)] = x_ref[pl.ds(me, 1)]
    every = pltpu.make_async_remote_copy(
        src_ref=x_ref.at[pl.ds(0, n - 1)],
        dst_ref=y_ref.at[pl.ds(0, n - 1)],
        send_sem=send_sem,
        recv_sem=recv_sem,
        device_id=where(lax.rem(me + 1, n)),
        device_id_type=MESH,
    )
    every.wait_send()
    every.wait_recv()


def exchange(x, n, width, cid):
    return pl.pallas_call(
        functools.partial(_a2a_kernel, n, width),
        out_shape=jax.ShapeDtypeStruct(x.shape, x.dtype),
        in_specs=[pl.BlockSpec(memory_space=pltpu.VMEM)],
        out_specs=pl.BlockSpec(memory_space=pltpu.VMEM),
        scratch_shapes=[pltpu.SemaphoreType.DMA, pltpu.SemaphoreType.DMA],
        compiler_params=pltpu.CompilerParams(collective_id=cid, has_side_effects=True),
    )(x)


def per_device(
    gradients,
    adam_mean,
    adam_square,
    stat_left,
    stat_right,
    root_left,
    root_right,
    owners,
    small_grad,
    small_mean,
    small_square,
):
    layer_count, row_count, col_count = gradients.shape
    block_count = col_count // BLOCK
    devices = lax.axis_size(("shard", "tensor"))
    width = lax.axis_size("tensor")
    slot_count = stat_left.shape[1]
    total_blocks = owners.shape[0]
    positions = jnp.arange(total_blocks, dtype=jnp.int32)
    earlier = (owners[:, None] == owners[None, :]) & (positions[None, :] < positions[:, None])
    slot_index = jnp.sum(earlier.astype(jnp.int32), axis=1)
    target = owners * slot_count + slot_index
    places = jnp.arange(devices * slot_count, dtype=jnp.int32)
    picker = (
        (places[:, None] == target[None, :])
        .astype(jnp.bfloat16)
        .reshape(devices * slot_count, layer_count, block_count)
    )
    grad_wide = gradients.astype(jnp.float32)
    mean_out, square_out, direction = adam_moments(grad_wide, adam_mean, adam_square)
    adam_part = jnp.sum(
        jnp.square(direction).reshape(layer_count, row_count, block_count, BLOCK), axis=(1, 3)
    )
    part_by_place = (
        jnp.zeros((devices * slot_count,), jnp.float32)
        .at[target]
        .set(adam_part.reshape(total_blocks))
        .reshape(devices, slot_count)
    )
    part_hi = part_by_place.astype(jnp.bfloat16)
    part_lo = (part_by_place - part_hi.astype(jnp.float32)).astype(jnp.bfloat16)
    extra_rows = 16 - slot_count * row_count
    pad = ((0, 0), (0, BLOCK - slot_count))
    extra = jnp.stack(
        [jnp.pad(part_hi, pad), jnp.pad(part_lo, pad)]
        + [jnp.zeros((devices, BLOCK), jnp.bfloat16)] * (extra_rows - 2),
        axis=1,
    )
    pieces = gradients.reshape(layer_count, row_count, block_count, BLOCK)
    outgoing = jnp.einsum(
        "qln,lrnb->qrb", picker, pieces, preferred_element_type=jnp.float32
    ).astype(jnp.bfloat16)
    outgoing = jnp.concatenate(
        [outgoing.reshape(devices, slot_count * row_count, BLOCK), extra], axis=1
    )
    incoming = exchange(outgoing, devices, width, 0)
    block_grads = (
        incoming[:, : slot_count * row_count]
        .reshape(devices, slot_count, row_count, BLOCK)
        .transpose(1, 0, 2, 3)
        .reshape(slot_count, devices * row_count, BLOCK)
    )
    tail = slot_count * row_count
    adam_sums = jnp.sum(
        incoming[:, tail, :slot_count].astype(jnp.float32)
        + incoming[:, tail + 1, :slot_count].astype(jnp.float32),
        axis=0,
    )
    left_out = (
        stat_left
        + jnp.einsum("cib,cjb->cij", block_grads, block_grads, preferred_element_type=jnp.float32)[
            None
        ]
    )
    right_out = (
        stat_right
        + jnp.einsum("cib,cid->cbd", block_grads, block_grads, preferred_element_type=jnp.float32)[
            None
        ]
    )
    left_applied = jnp.einsum(
        "cij,cjb->cib", root_left[0], block_grads.astype(jnp.float32), precision=PRECISE
    )
    precond = jnp.einsum("cib,cbd->cid", left_applied, root_right[0], precision=PRECISE)
    precond_sums = jnp.sum(jnp.square(precond), axis=(1, 2))
    graft_ratio = jnp.sqrt(adam_sums / (precond_sums + 1e-06))
    scaled = precond * graft_ratio[:, None, None]
    shaped = (
        scaled.reshape(slot_count, devices, row_count, BLOCK)
        .transpose(1, 0, 2, 3)
        .reshape(devices, slot_count * row_count, BLOCK)
    )
    returned = exchange(shaped, devices, width, 1)
    returned = returned.reshape(devices * slot_count, row_count, BLOCK)
    own_rows = jnp.take(returned, target, axis=0).reshape(
        layer_count, block_count, row_count, BLOCK
    )
    updates = own_rows.transpose(0, 2, 1, 3).reshape(layer_count, row_count, col_count)
    small_mean_out, small_square_out, small_update = adam_moments(
        small_grad, small_mean, small_square
    )
    return (
        updates,
        mean_out,
        square_out,
        left_out,
        right_out,
        small_update,
        small_mean_out,
        small_square_out,
    )


def solution(mesh):
    in_specs = (
        P(None, ("shard", "tensor"), None),
        P(None, ("shard", "tensor"), None),
        P(None, ("shard", "tensor"), None),
        P(("shard", "tensor"), None, None, None),
        P(("shard", "tensor"), None, None, None),
        P(("shard", "tensor"), None, None, None),
        P(("shard", "tensor"), None, None, None),
        P(),
        P(),
        P(),
        P(),
    )
    out_specs = (
        P(None, ("shard", "tensor"), None),
        P(None, ("shard", "tensor"), None),
        P(None, ("shard", "tensor"), None),
        P(("shard", "tensor"), None, None, None),
        P(("shard", "tensor"), None, None, None),
        P(),
        P(),
        P(),
    )
    return jax.shard_map(
        per_device, mesh=mesh, in_specs=in_specs, out_specs=out_specs, check_vma=False
    )
```

```python
import functools

import jax
import jax.numpy as jnp
from jax import lax
from jax.experimental import pallas as pl
from jax.experimental.pallas import tpu as pltpu
from jax.sharding import PartitionSpec as P

BLOCK = 128
MESH = pl.DeviceIdType.MESH


PRECISE = lax.Precision.HIGHEST


def adam_moments(grad_wide, mean_old, square_old):
    mean_new = 0.9 * mean_old + 0.1 * grad_wide
    square_new = 0.95 * square_old + 0.05 * grad_wide * grad_wide
    return (mean_new, square_new, mean_new / (jnp.sqrt(square_new) + 1e-08))


def _a2a_kernel(S, W, x_ref, w_ref, z_ref, s1, r1, s2, r2, l1, l2):
    s = lax.axis_index("shard")
    t = lax.axis_index("tensor")
    barrier = pltpu.get_barrier_semaphore()
    for j in range(1, W):
        pl.semaphore_signal(barrier, inc=1, device_id=(s, lax.rem(t + j, W)), device_id_type=MESH)
    for j in range(1, S):
        pl.semaphore_signal(barrier, inc=1, device_id=(lax.rem(s + j, S), t), device_id_type=MESH)
    pl.semaphore_wait(barrier, W - 1 + S - 1)
    for j in range(1, W):
        tp = lax.rem(t + j, W)
        pltpu.make_async_remote_copy(
            src_ref=x_ref.at[tp], dst_ref=z_ref.at[t], send_sem=s1, recv_sem=r1,
            device_id=(s, tp), device_id_type=MESH,
        ).start()
    near = pltpu.make_async_copy(x_ref.at[t], z_ref.at[t], l1)
    near.start()
    first = pltpu.make_async_remote_copy(
        src_ref=x_ref.at[pl.ds(0, W - 1)], dst_ref=z_ref.at[pl.ds(0, W - 1)], send_sem=s1, recv_sem=r1,
        device_id=(s, lax.rem(t + 1, W)), device_id_type=MESH,
    )
    near.wait()
    first.wait_send()
    first.wait_recv()
    for j in range(1, S):
        sp = lax.rem(s + j, S)
        pltpu.make_async_remote_copy(
            src_ref=z_ref.at[:, sp], dst_ref=w_ref.at[s], send_sem=s2, recv_sem=r2,
            device_id=(sp, t), device_id_type=MESH,
        ).start()
    home = pltpu.make_async_copy(z_ref.at[:, s], w_ref.at[s], l2)
    home.start()
    second = pltpu.make_async_remote_copy(
        src_ref=w_ref.at[pl.ds(0, S - 1)], dst_ref=w_ref.at[pl.ds(0, S - 1)], send_sem=s2, recv_sem=r2,
        device_id=(lax.rem(s + 1, S), t), device_id_type=MESH,
    )
    home.wait()
    second.wait_send()
    second.wait_recv()


def exchange(x, S, W, cid):
    n, rows, lanes = x.shape
    xt = x.reshape(S, W, rows, lanes).transpose(1, 0, 2, 3)
    w = pl.pallas_call(
        functools.partial(_a2a_kernel, S, W),
        out_shape=jax.ShapeDtypeStruct((S, W, rows, lanes), x.dtype),
        in_specs=[pl.BlockSpec(memory_space=pltpu.VMEM)],
        out_specs=pl.BlockSpec(memory_space=pltpu.VMEM),
        scratch_shapes=[pltpu.VMEM((W, S, rows, lanes), x.dtype)] + [pltpu.SemaphoreType.DMA] * 6,
        compiler_params=pltpu.CompilerParams(collective_id=cid, has_side_effects=True),
    )(xt)
    return w.reshape(n, rows, lanes)


def per_device(
    gradients,
    adam_mean,
    adam_square,
    stat_left,
    stat_right,
    root_left,
    root_right,
    owners,
    small_grad,
    small_mean,
    small_square,
):
    layer_count, row_count, col_count = gradients.shape
    block_count = col_count // BLOCK
    devices = lax.axis_size(("shard", "tensor"))
    width = lax.axis_size("tensor")
    height = lax.axis_size("shard")
    slot_count = stat_left.shape[1]
    total_blocks = owners.shape[0]
    positions = jnp.arange(total_blocks, dtype=jnp.int32)
    earlier = (owners[:, None] == owners[None, :]) & (positions[None, :] < positions[:, None])
    slot_index = jnp.sum(earlier.astype(jnp.int32), axis=1)
    target = owners * slot_count + slot_index
    places = jnp.arange(devices * slot_count, dtype=jnp.int32)
    picker = (
        (places[:, None] == target[None, :])
        .astype(jnp.bfloat16)
        .reshape(devices * slot_count, layer_count, block_count)
    )
    grad_wide = gradients.astype(jnp.float32)
    mean_out, square_out, direction = adam_moments(grad_wide, adam_mean, adam_square)
    adam_part = jnp.sum(
        jnp.square(direction).reshape(layer_count, row_count, block_count, BLOCK), axis=(1, 3)
    )
    part_by_place = (
        jnp.zeros((devices * slot_count,), jnp.float32)
        .at[target]
        .set(adam_part.reshape(total_blocks))
        .reshape(devices, slot_count)
    )
    part_hi = part_by_place.astype(jnp.bfloat16)
    part_lo = (part_by_place - part_hi.astype(jnp.float32)).astype(jnp.bfloat16)
    extra_rows = 16 - slot_count * row_count
    pad = ((0, 0), (0, BLOCK - slot_count))
    extra = jnp.stack(
        [jnp.pad(part_hi, pad), jnp.pad(part_lo, pad)]
        + [jnp.zeros((devices, BLOCK), jnp.bfloat16)] * (extra_rows - 2),
        axis=1,
    )
    pieces = gradients.reshape(layer_count, row_count, block_count, BLOCK)
    outgoing = jnp.einsum(
        "qln,lrnb->qrb", picker, pieces, preferred_element_type=jnp.float32
    ).astype(jnp.bfloat16)
    outgoing = jnp.concatenate(
        [outgoing.reshape(devices, slot_count * row_count, BLOCK), extra], axis=1
    )
    incoming = exchange(outgoing, height, width, 0)
    block_grads = (
        incoming[:, : slot_count * row_count]
        .reshape(devices, slot_count, row_count, BLOCK)
        .transpose(1, 0, 2, 3)
        .reshape(slot_count, devices * row_count, BLOCK)
    )
    tail = slot_count * row_count
    adam_sums = jnp.sum(
        incoming[:, tail, :slot_count].astype(jnp.float32)
        + incoming[:, tail + 1, :slot_count].astype(jnp.float32),
        axis=0,
    )
    left_out = (
        stat_left
        + jnp.einsum("cib,cjb->cij", block_grads, block_grads, preferred_element_type=jnp.float32)[
            None
        ]
    )
    right_out = (
        stat_right
        + jnp.einsum("cib,cid->cbd", block_grads, block_grads, preferred_element_type=jnp.float32)[
            None
        ]
    )
    left_applied = jnp.einsum(
        "cij,cjb->cib", root_left[0], block_grads.astype(jnp.float32), precision=PRECISE
    )
    precond = jnp.einsum("cib,cbd->cid", left_applied, root_right[0], precision=PRECISE)
    precond_sums = jnp.sum(jnp.square(precond), axis=(1, 2))
    graft_ratio = jnp.sqrt(adam_sums / (precond_sums + 1e-06))
    scaled = precond * graft_ratio[:, None, None]
    shaped = (
        scaled.reshape(slot_count, devices, row_count, BLOCK)
        .transpose(1, 0, 2, 3)
        .reshape(devices, slot_count * row_count, BLOCK)
    )
    returned = exchange(shaped, height, width, 1)
    returned = returned.reshape(devices * slot_count, row_count, BLOCK)
    own_rows = jnp.take(returned, target, axis=0).reshape(
        layer_count, block_count, row_count, BLOCK
    )
    updates = own_rows.transpose(0, 2, 1, 3).reshape(layer_count, row_count, col_count)
    small_mean_out, small_square_out, small_update = adam_moments(
        small_grad, small_mean, small_square
    )
    return (
        updates,
        mean_out,
        square_out,
        left_out,
        right_out,
        small_update,
        small_mean_out,
        small_square_out,
    )


def solution(mesh):
    in_specs = (
        P(None, ("shard", "tensor"), None),
        P(None, ("shard", "tensor"), None),
        P(None, ("shard", "tensor"), None),
        P(("shard", "tensor"), None, None, None),
        P(("shard", "tensor"), None, None, None),
        P(("shard", "tensor"), None, None, None),
        P(("shard", "tensor"), None, None, None),
        P(),
        P(),
        P(),
        P(),
    )
    out_specs = (
        P(None, ("shard", "tensor"), None),
        P(None, ("shard", "tensor"), None),
        P(None, ("shard", "tensor"), None),
        P(("shard", "tensor"), None, None, None),
        P(("shard", "tensor"), None, None, None),
        P(),
        P(),
        P(),
    )
    return jax.shard_map(
        per_device, mesh=mesh, in_specs=in_specs, out_specs=out_specs, check_vma=False
    )
```

```python
import jax
import jax.numpy as jnp
from jax import lax
from jax.sharding import PartitionSpec as P

BLOCK = 128


PRECISE = lax.Precision.HIGHEST


def adam_moments(grad_wide, mean_old, square_old):
    mean_new = 0.9 * mean_old + 0.1 * grad_wide
    square_new = 0.95 * square_old + 0.05 * grad_wide * grad_wide
    return (mean_new, square_new, mean_new / (jnp.sqrt(square_new) + 1e-08))


def per_device(
    gradients,
    adam_mean,
    adam_square,
    stat_left,
    stat_right,
    root_left,
    root_right,
    owners,
    small_grad,
    small_mean,
    small_square,
):
    layer_count, row_count, col_count = gradients.shape
    block_count = col_count // BLOCK
    devices = lax.axis_size(("shard", "tensor"))
    slot_count = stat_left.shape[1]
    total_blocks = owners.shape[0]
    positions = jnp.arange(total_blocks, dtype=jnp.int32)
    earlier = (owners[:, None] == owners[None, :]) & (positions[None, :] < positions[:, None])
    slot_index = jnp.sum(earlier.astype(jnp.int32), axis=1)
    target = slot_index * devices + owners
    places = jnp.arange(slot_count * devices, dtype=jnp.int32)
    picker = (
        (places[:, None] == target[None, :])
        .astype(jnp.bfloat16)
        .reshape(slot_count * devices, layer_count, block_count)
    )
    grad_wide = gradients.astype(jnp.float32)
    mean_out, square_out, direction = adam_moments(grad_wide, adam_mean, adam_square)
    adam_part = jnp.sum(
        jnp.square(direction).reshape(layer_count, row_count, block_count, BLOCK), axis=(1, 3)
    )
    pieces = gradients.reshape(layer_count, row_count, block_count, BLOCK)
    outgoing = jnp.einsum(
        "qln,lrnb->qrb", picker, pieces, preferred_element_type=jnp.float32
    ).astype(jnp.bfloat16)
    outgoing = outgoing.reshape(slot_count, devices, row_count, BLOCK)
    incoming = lax.all_to_all(
        outgoing, ("shard", "tensor"), split_axis=1, concat_axis=1, tiled=True
    )
    block_grads = incoming.reshape(slot_count, devices * row_count, BLOCK)
    gathered = lax.all_gather(adam_part.reshape(total_blocks), ("shard", "tensor"))
    block_sums = jnp.sum(gathered, axis=0)
    me = lax.axis_index(("shard", "tensor"))
    place_sums = (
        jnp.zeros((slot_count * devices,), jnp.float32)
        .at[target]
        .set(block_sums)
        .reshape(slot_count, devices)
    )
    adam_sums = lax.dynamic_index_in_dim(place_sums, me, axis=1, keepdims=False)
    left_out = (
        stat_left
        + jnp.einsum("cib,cjb->cij", block_grads, block_grads, preferred_element_type=jnp.float32)[
            None
        ]
    )
    right_out = (
        stat_right
        + jnp.einsum("cib,cid->cbd", block_grads, block_grads, preferred_element_type=jnp.float32)[
            None
        ]
    )
    left_applied = jnp.einsum(
        "cij,cjb->cib", root_left[0], block_grads.astype(jnp.float32), precision=PRECISE
    )
    precond = jnp.einsum("cib,cbd->cid", left_applied, root_right[0], precision=PRECISE)
    precond_sums = jnp.sum(jnp.square(precond), axis=(1, 2))
    graft_ratio = jnp.sqrt(adam_sums / (precond_sums + 1e-06))
    scaled = precond * graft_ratio[:, None, None]
    shaped = scaled.reshape(slot_count, devices, row_count, BLOCK)
    returned = lax.all_to_all(shaped, ("shard", "tensor"), split_axis=1, concat_axis=1, tiled=True)
    returned = returned.reshape(slot_count * devices, row_count, BLOCK)
    own_rows = jnp.take(returned, target, axis=0).reshape(
        layer_count, block_count, row_count, BLOCK
    )
    updates = own_rows.transpose(0, 2, 1, 3).reshape(layer_count, row_count, col_count)
    small_mean_out, small_square_out, small_update = adam_moments(
        small_grad, small_mean, small_square
    )
    return (
        updates,
        mean_out,
        square_out,
        left_out,
        right_out,
        small_update,
        small_mean_out,
        small_square_out,
    )


def solution(mesh):
    in_specs = (
        P(None, ("shard", "tensor"), None),
        P(None, ("shard", "tensor"), None),
        P(None, ("shard", "tensor"), None),
        P(("shard", "tensor"), None, None, None),
        P(("shard", "tensor"), None, None, None),
        P(("shard", "tensor"), None, None, None),
        P(("shard", "tensor"), None, None, None),
        P(),
        P(),
        P(),
        P(),
    )
    out_specs = (
        P(None, ("shard", "tensor"), None),
        P(None, ("shard", "tensor"), None),
        P(None, ("shard", "tensor"), None),
        P(("shard", "tensor"), None, None, None),
        P(("shard", "tensor"), None, None, None),
        P(),
        P(),
        P(),
    )
    return jax.shard_map(
        per_device, mesh=mesh, in_specs=in_specs, out_specs=out_specs, check_vma=False
    )
```

```python
import jax
import jax.numpy as jnp
from jax import lax
from jax.sharding import PartitionSpec as P

BLOCK = 128


PRECISE = lax.Precision.HIGHEST


def adam_moments(grad_wide, mean_old, square_old):
    mean_new = 0.9 * mean_old + 0.1 * grad_wide
    square_new = 0.95 * square_old + 0.05 * grad_wide * grad_wide
    return (mean_new, square_new, mean_new / (jnp.sqrt(square_new) + 1e-08))


def exchange(x):
    return lax.all_to_all(x, ("shard", "tensor"), split_axis=0, concat_axis=0, tiled=True)


def per_device(
    gradients,
    adam_mean,
    adam_square,
    stat_left,
    stat_right,
    root_left,
    root_right,
    owners,
    small_grad,
    small_mean,
    small_square,
):
    layer_count, row_count, col_count = gradients.shape
    block_count = col_count // BLOCK
    devices = lax.axis_size(("shard", "tensor"))
    slot_count = stat_left.shape[1]
    total_blocks = owners.shape[0]
    positions = jnp.arange(total_blocks, dtype=jnp.int32)
    earlier = (owners[:, None] == owners[None, :]) & (positions[None, :] < positions[:, None])
    slot_index = jnp.sum(earlier.astype(jnp.int32), axis=1)
    target = owners * slot_count + slot_index
    places = jnp.arange(devices * slot_count, dtype=jnp.int32)
    picker = (
        (places[:, None] == target[None, :])
        .astype(jnp.bfloat16)
        .reshape(devices * slot_count, layer_count, block_count)
    )
    grad_wide = gradients.astype(jnp.float32)
    mean_out, square_out, direction = adam_moments(grad_wide, adam_mean, adam_square)
    adam_part = jnp.sum(
        jnp.square(direction).reshape(layer_count, row_count, block_count, BLOCK), axis=(1, 3)
    )
    part_by_place = (
        jnp.zeros((devices * slot_count,), jnp.float32)
        .at[target]
        .set(adam_part.reshape(total_blocks))
        .reshape(devices, slot_count)
    )
    part_hi = part_by_place.astype(jnp.bfloat16)
    part_lo = (part_by_place - part_hi.astype(jnp.float32)).astype(jnp.bfloat16)
    extra_rows = 16 - slot_count * row_count
    pad = ((0, 0), (0, BLOCK - slot_count))
    extra = jnp.stack(
        [jnp.pad(part_hi, pad), jnp.pad(part_lo, pad)]
        + [jnp.zeros((devices, BLOCK), jnp.bfloat16)] * (extra_rows - 2),
        axis=1,
    )
    pieces = gradients.reshape(layer_count, row_count, block_count, BLOCK)
    outgoing = jnp.einsum(
        "qln,lrnb->qrb", picker, pieces, preferred_element_type=jnp.float32
    ).astype(jnp.bfloat16)
    outgoing = jnp.concatenate(
        [outgoing.reshape(devices, slot_count * row_count, BLOCK), extra], axis=1
    )
    incoming = exchange(outgoing)
    block_grads = (
        incoming[:, : slot_count * row_count]
        .reshape(devices, slot_count, row_count, BLOCK)
        .transpose(1, 0, 2, 3)
        .reshape(slot_count, devices * row_count, BLOCK)
    )
    tail = slot_count * row_count
    adam_sums = jnp.sum(
        incoming[:, tail, :slot_count].astype(jnp.float32)
        + incoming[:, tail + 1, :slot_count].astype(jnp.float32),
        axis=0,
    )
    left_out = (
        stat_left
        + jnp.einsum("cib,cjb->cij", block_grads, block_grads, preferred_element_type=jnp.float32)[
            None
        ]
    )
    right_out = (
        stat_right
        + jnp.einsum("cib,cid->cbd", block_grads, block_grads, preferred_element_type=jnp.float32)[
            None
        ]
    )
    left_applied = jnp.einsum(
        "cij,cjb->cib", root_left[0], block_grads.astype(jnp.float32), precision=PRECISE
    )
    precond = jnp.einsum("cib,cbd->cid", left_applied, root_right[0], precision=PRECISE)
    precond_sums = jnp.sum(jnp.square(precond), axis=(1, 2))
    graft_ratio = jnp.sqrt(adam_sums / (precond_sums + 1e-06))
    scaled = precond * graft_ratio[:, None, None]
    shaped = (
        scaled.reshape(slot_count, devices, row_count, BLOCK)
        .transpose(1, 0, 2, 3)
        .reshape(devices, slot_count * row_count, BLOCK)
    )
    returned = exchange(shaped)
    returned = returned.reshape(devices * slot_count, row_count, BLOCK)
    own_rows = jnp.take(returned, target, axis=0).reshape(
        layer_count, block_count, row_count, BLOCK
    )
    updates = own_rows.transpose(0, 2, 1, 3).reshape(layer_count, row_count, col_count)
    small_mean_out, small_square_out, small_update = adam_moments(
        small_grad, small_mean, small_square
    )
    return (
        updates,
        mean_out,
        square_out,
        left_out,
        right_out,
        small_update,
        small_mean_out,
        small_square_out,
    )


def solution(mesh):
    in_specs = (
        P(None, ("shard", "tensor"), None),
        P(None, ("shard", "tensor"), None),
        P(None, ("shard", "tensor"), None),
        P(("shard", "tensor"), None, None, None),
        P(("shard", "tensor"), None, None, None),
        P(("shard", "tensor"), None, None, None),
        P(("shard", "tensor"), None, None, None),
        P(),
        P(),
        P(),
        P(),
    )
    out_specs = (
        P(None, ("shard", "tensor"), None),
        P(None, ("shard", "tensor"), None),
        P(None, ("shard", "tensor"), None),
        P(("shard", "tensor"), None, None, None),
        P(("shard", "tensor"), None, None, None),
        P(),
        P(),
        P(),
    )
    return jax.shard_map(
        per_device, mesh=mesh, in_specs=in_specs, out_specs=out_specs, check_vma=False
    )
```

```python
import jax
import jax.numpy as jnp
from jax import lax
from jax.sharding import PartitionSpec as P

BLOCK = 128


PRECISE = lax.Precision.HIGHEST


def adam_moments(grad_wide, mean_old, square_old):
    mean_new = 0.9 * mean_old + 0.1 * grad_wide
    square_new = 0.95 * square_old + 0.05 * grad_wide * grad_wide
    return (mean_new, square_new, mean_new / (jnp.sqrt(square_new) + 1e-08))


def exchange(x):
    return lax.all_to_all(x, ("shard", "tensor"), split_axis=0, concat_axis=0, tiled=True)


def per_device(
    gradients,
    adam_mean,
    adam_square,
    stat_left,
    stat_right,
    root_left,
    root_right,
    owners,
    small_grad,
    small_mean,
    small_square,
):
    layer_count, row_count, col_count = gradients.shape
    block_count = col_count // BLOCK
    devices = lax.axis_size(("shard", "tensor"))
    slot_count = stat_left.shape[1]
    total_blocks = owners.shape[0]
    positions = jnp.arange(total_blocks, dtype=jnp.int32)
    earlier = (owners[:, None] == owners[None, :]) & (positions[None, :] < positions[:, None])
    slot_index = jnp.sum(earlier.astype(jnp.int32), axis=1)
    target = owners * slot_count + slot_index
    places = jnp.arange(devices * slot_count, dtype=jnp.int32)
    picker = (
        (places[:, None] == target[None, :])
        .astype(jnp.bfloat16)
        .reshape(devices * slot_count, layer_count, block_count)
    )
    grad_wide = gradients.astype(jnp.float32)
    mean_out, square_out, direction = adam_moments(grad_wide, adam_mean, adam_square)
    adam_part = jnp.sum(
        jnp.square(direction).reshape(layer_count, row_count, block_count, BLOCK), axis=(1, 3)
    )
    part_by_place = (
        jnp.zeros((devices * slot_count,), jnp.float32)
        .at[target]
        .set(adam_part.reshape(total_blocks))
        .reshape(devices, slot_count)
    )
    part_hi = part_by_place.astype(jnp.bfloat16)
    part_lo = (part_by_place - part_hi.astype(jnp.float32)).astype(jnp.bfloat16)
    extra_rows = 16 - slot_count * row_count
    pad = ((0, 0), (0, BLOCK - slot_count))
    extra = jnp.stack(
        [jnp.pad(part_hi, pad), jnp.pad(part_lo, pad)]
        + [jnp.zeros((devices, BLOCK), jnp.bfloat16)] * (extra_rows - 2),
        axis=1,
    )
    pieces = gradients.reshape(layer_count, row_count, block_count, BLOCK)
    outgoing = jnp.einsum(
        "qln,lrnb->qrb", picker, pieces, preferred_element_type=jnp.float32
    ).astype(jnp.bfloat16)
    outgoing = jnp.concatenate(
        [outgoing.reshape(devices, slot_count * row_count, BLOCK), extra], axis=1
    )
    incoming = exchange(outgoing)
    block_grads = (
        incoming[:, : slot_count * row_count]
        .reshape(devices, slot_count, row_count, BLOCK)
        .transpose(1, 0, 2, 3)
        .reshape(slot_count, devices * row_count, BLOCK)
    )
    tail = slot_count * row_count
    adam_sums = jnp.sum(
        incoming[:, tail, :slot_count].astype(jnp.float32)
        + incoming[:, tail + 1, :slot_count].astype(jnp.float32),
        axis=0,
    )
    left_out = (
        stat_left
        + jnp.einsum("cib,cjb->cij", block_grads, block_grads, preferred_element_type=jnp.float32)[
            None
        ]
    )
    right_out = (
        stat_right
        + jnp.einsum("cib,cid->cbd", block_grads, block_grads, preferred_element_type=jnp.float32)[
            None
        ]
    )
    left_applied = jnp.einsum(
        "cij,cjb->cib", root_left[0], block_grads.astype(jnp.float32), precision=PRECISE
    )
    precond = jnp.einsum("cib,cbd->cid", left_applied, root_right[0], precision=PRECISE)
    precond_sums = jnp.sum(jnp.square(precond), axis=(1, 2))
    graft_ratio = jnp.sqrt(adam_sums / (precond_sums + 1e-06))
    scaled = precond * graft_ratio[:, None, None]
    shaped = scaled.reshape(slot_count, devices, row_count, BLOCK).transpose(1, 0, 2, 3)
    returned = exchange(shaped).reshape(devices * slot_count, row_count, BLOCK)
    rows = jnp.arange(row_count, dtype=jnp.int32)
    updates = returned[
        target.reshape(layer_count, 1, block_count), rows[None, :, None]
    ].reshape(layer_count, row_count, col_count)
    small_mean_out, small_square_out, small_update = adam_moments(
        small_grad, small_mean, small_square
    )
    return (
        updates,
        mean_out,
        square_out,
        left_out,
        right_out,
        small_update,
        small_mean_out,
        small_square_out,
    )


def solution(mesh):
    in_specs = (
        P(None, ("shard", "tensor"), None),
        P(None, ("shard", "tensor"), None),
        P(None, ("shard", "tensor"), None),
        P(("shard", "tensor"), None, None, None),
        P(("shard", "tensor"), None, None, None),
        P(("shard", "tensor"), None, None, None),
        P(("shard", "tensor"), None, None, None),
        P(),
        P(),
        P(),
        P(),
    )
    out_specs = (
        P(None, ("shard", "tensor"), None),
        P(None, ("shard", "tensor"), None),
        P(None, ("shard", "tensor"), None),
        P(("shard", "tensor"), None, None, None),
        P(("shard", "tensor"), None, None, None),
        P(),
        P(),
        P(),
    )
    return jax.shard_map(
        per_device, mesh=mesh, in_specs=in_specs, out_specs=out_specs, check_vma=False
    )
```

```python
import jax
import jax.numpy as jnp
from jax import lax
from jax.sharding import PartitionSpec as P

BLOCK = 128


PRECISE = lax.Precision.HIGHEST


def adam_moments(grad_wide, mean_old, square_old):
    mean_new = 0.9 * mean_old + 0.1 * grad_wide
    square_new = 0.95 * square_old + 0.05 * grad_wide * grad_wide
    return (mean_new, square_new, mean_new / (jnp.sqrt(square_new) + 1e-08))


def per_device(
    gradients,
    adam_mean,
    adam_square,
    stat_left,
    stat_right,
    root_left,
    root_right,
    owners,
    small_grad,
    small_mean,
    small_square,
):
    layer_count, row_count, col_count = gradients.shape
    block_count = col_count // BLOCK
    devices = lax.axis_size(("shard", "tensor"))
    slot_count = stat_left.shape[1]
    total_blocks = owners.shape[0]
    positions = jnp.arange(total_blocks, dtype=jnp.int32)
    earlier = (owners[:, None] == owners[None, :]) & (positions[None, :] < positions[:, None])
    slot_index = jnp.sum(earlier.astype(jnp.int32), axis=1)
    target = slot_index * devices + owners
    sent_to = owners * slot_count + slot_index
    places = jnp.arange(slot_count * devices, dtype=jnp.int32)
    picker = (
        (places[:, None] == sent_to[None, :])
        .astype(jnp.bfloat16)
        .reshape(slot_count * devices, layer_count, block_count)
    )
    grad_wide = gradients.astype(jnp.float32)
    mean_out, square_out, direction = adam_moments(grad_wide, adam_mean, adam_square)
    adam_part = jnp.sum(
        jnp.square(direction).reshape(layer_count, row_count, block_count, BLOCK), axis=(1, 3)
    )
    part_hi = adam_part.astype(jnp.bfloat16)
    part_lo = (adam_part - part_hi.astype(jnp.float32)).astype(jnp.bfloat16)
    lane = jnp.arange(BLOCK, dtype=jnp.int32)
    extra = jnp.where(
        lane == 0,
        part_hi[:, :, None],
        jnp.where(lane == 1, part_lo[:, :, None], jnp.zeros((), jnp.bfloat16)),
    )[:, None]
    pieces = jnp.concatenate(
        [gradients.reshape(layer_count, row_count, block_count, BLOCK), extra], axis=1
    )
    outgoing = jnp.einsum(
        "qln,lrnb->qrb", picker, pieces, preferred_element_type=jnp.float32
    ).astype(jnp.bfloat16)
    chunk = slot_count * (row_count + 1)
    chunk_rows = -(-chunk // 16) * 16
    outgoing = jnp.pad(
        outgoing.reshape(devices, chunk, BLOCK), ((0, 0), (0, chunk_rows - chunk), (0, 0))
    )
    incoming = lax.all_to_all(
        outgoing, ("shard", "tensor"), split_axis=0, concat_axis=0, tiled=True
    )
    incoming = incoming[:, :chunk].reshape(devices, slot_count, row_count + 1, BLOCK)
    block_grads = (
        incoming[:, :, :row_count]
        .transpose(1, 0, 2, 3)
        .reshape(slot_count, devices * row_count, BLOCK)
    )
    adam_sums = jnp.sum(
        incoming[:, :, row_count, 0].astype(jnp.float32)
        + incoming[:, :, row_count, 1].astype(jnp.float32),
        axis=0,
    )
    left_out = (
        stat_left
        + jnp.einsum("cib,cjb->cij", block_grads, block_grads, preferred_element_type=jnp.float32)[
            None
        ]
    )
    right_out = (
        stat_right
        + jnp.einsum("cib,cid->cbd", block_grads, block_grads, preferred_element_type=jnp.float32)[
            None
        ]
    )
    left_applied = jnp.einsum(
        "cij,cjb->cib", root_left[0], block_grads.astype(jnp.float32), precision=PRECISE
    )
    precond = jnp.einsum("cib,cbd->cid", left_applied, root_right[0], precision=PRECISE)
    precond_sums = jnp.sum(jnp.square(precond), axis=(1, 2))
    graft_ratio = jnp.sqrt(adam_sums / (precond_sums + 1e-06))
    scaled = precond * graft_ratio[:, None, None]
    shaped = scaled.reshape(slot_count, devices, row_count, BLOCK)
    returned = lax.all_to_all(shaped, ("shard", "tensor"), split_axis=1, concat_axis=1, tiled=True)
    returned = returned.reshape(slot_count * devices, row_count, BLOCK)
    own_rows = jnp.take(returned, target, axis=0).reshape(
        layer_count, block_count, row_count, BLOCK
    )
    updates = own_rows.transpose(0, 2, 1, 3).reshape(layer_count, row_count, col_count)
    small_mean_out, small_square_out, small_update = adam_moments(
        small_grad, small_mean, small_square
    )
    return (
        updates,
        mean_out,
        square_out,
        left_out,
        right_out,
        small_update,
        small_mean_out,
        small_square_out,
    )


def solution(mesh):
    in_specs = (
        P(None, ("shard", "tensor"), None),
        P(None, ("shard", "tensor"), None),
        P(None, ("shard", "tensor"), None),
        P(("shard", "tensor"), None, None, None),
        P(("shard", "tensor"), None, None, None),
        P(("shard", "tensor"), None, None, None),
        P(("shard", "tensor"), None, None, None),
        P(),
        P(),
        P(),
        P(),
    )
    out_specs = (
        P(None, ("shard", "tensor"), None),
        P(None, ("shard", "tensor"), None),
        P(None, ("shard", "tensor"), None),
        P(("shard", "tensor"), None, None, None),
        P(("shard", "tensor"), None, None, None),
        P(),
        P(),
        P(),
    )
    return jax.shard_map(
        per_device, mesh=mesh, in_specs=in_specs, out_specs=out_specs, check_vma=False
    )
```

```python
import jax
import jax.numpy as jnp
from jax import lax
from jax.sharding import PartitionSpec as P

BLOCK = 128


PRECISE = lax.Precision.HIGHEST


def adam_moments(grad_wide, mean_old, square_old):
    mean_new = 0.9 * mean_old + 0.1 * grad_wide
    square_new = 0.95 * square_old + 0.05 * grad_wide * grad_wide
    return (mean_new, square_new, mean_new / (jnp.sqrt(square_new) + 1e-08))


def per_device(
    gradients,
    adam_mean,
    adam_square,
    stat_left,
    stat_right,
    root_left,
    root_right,
    owners,
    small_grad,
    small_mean,
    small_square,
):
    layer_count, row_count, col_count = gradients.shape
    block_count = col_count // BLOCK
    devices = lax.axis_size(("shard", "tensor"))
    slot_count = stat_left.shape[1]
    total_blocks = owners.shape[0]
    positions = jnp.arange(total_blocks, dtype=jnp.int32)
    earlier = (owners[:, None] == owners[None, :]) & (positions[None, :] < positions[:, None])
    slot_index = jnp.sum(earlier.astype(jnp.int32), axis=1)
    target = slot_index * devices + owners
    places = jnp.arange(slot_count * devices, dtype=jnp.int32)
    picker = (
        (places[:, None] == target[None, :])
        .astype(jnp.bfloat16)
        .reshape(slot_count * devices, layer_count, block_count)
    )
    grad_wide = gradients.astype(jnp.float32)
    mean_out, square_out, direction = adam_moments(grad_wide, adam_mean, adam_square)
    adam_part = jnp.sum(
        jnp.square(direction).reshape(layer_count, row_count, block_count, BLOCK), axis=(1, 3)
    )
    part_by_place = jnp.zeros((slot_count * devices,), jnp.float32).at[target].set(
        adam_part.reshape(total_blocks)
    )
    part_hi = part_by_place.astype(jnp.bfloat16)
    part_lo = (part_by_place - part_hi.astype(jnp.float32)).astype(jnp.bfloat16)
    lane = jnp.arange(BLOCK, dtype=jnp.int32)
    extra = jnp.where(
        lane[None, :] == 0,
        part_hi[:, None],
        jnp.where(lane[None, :] == 1, part_lo[:, None], jnp.zeros((), jnp.bfloat16)),
    )[:, None, :]
    pieces = gradients.reshape(layer_count, row_count, block_count, BLOCK)
    outgoing = jnp.einsum(
        "qln,lrnb->qrb", picker, pieces, preferred_element_type=jnp.float32
    ).astype(jnp.bfloat16)
    outgoing = jnp.concatenate([outgoing, extra], axis=1)
    outgoing = outgoing.reshape(slot_count, devices, row_count + 1, BLOCK)
    incoming = lax.all_to_all(
        outgoing, ("shard", "tensor"), split_axis=1, concat_axis=1, tiled=True
    )
    block_grads = incoming[:, :, :row_count, :].reshape(slot_count, devices * row_count, BLOCK)
    adam_sums = jnp.sum(
        incoming[:, :, row_count, 0].astype(jnp.float32)
        + incoming[:, :, row_count, 1].astype(jnp.float32),
        axis=1,
    )
    left_out = (
        stat_left
        + jnp.einsum("cib,cjb->cij", block_grads, block_grads, preferred_element_type=jnp.float32)[
            None
        ]
    )
    right_out = (
        stat_right
        + jnp.einsum("cib,cid->cbd", block_grads, block_grads, preferred_element_type=jnp.float32)[
            None
        ]
    )
    left_applied = jnp.einsum(
        "cij,cjb->cib", root_left[0], block_grads.astype(jnp.float32), precision=PRECISE
    )
    precond = jnp.einsum("cib,cbd->cid", left_applied, root_right[0], precision=PRECISE)
    precond_sums = jnp.sum(jnp.square(precond), axis=(1, 2))
    graft_ratio = jnp.sqrt(adam_sums / (precond_sums + 1e-06))
    scaled = precond * graft_ratio[:, None, None]
    shaped = scaled.reshape(slot_count, devices, row_count, BLOCK)
    returned = lax.all_to_all(shaped, ("shard", "tensor"), split_axis=1, concat_axis=1, tiled=True)
    placer = (
        (target[:, None] == places[None, :])
        .astype(jnp.float32)
        .reshape(layer_count, block_count, slot_count, devices)
    )
    updates = jnp.einsum(
        "lnqd,qdrb->lrnb", placer, returned, precision=PRECISE,
        preferred_element_type=jnp.float32,
    ).reshape(layer_count, row_count, col_count)
    small_mean_out, small_square_out, small_update = adam_moments(
        small_grad, small_mean, small_square
    )
    return (
        updates,
        mean_out,
        square_out,
        left_out,
        right_out,
        small_update,
        small_mean_out,
        small_square_out,
    )


def solution(mesh):
    in_specs = (
        P(None, ("shard", "tensor"), None),
        P(None, ("shard", "tensor"), None),
        P(None, ("shard", "tensor"), None),
        P(("shard", "tensor"), None, None, None),
        P(("shard", "tensor"), None, None, None),
        P(("shard", "tensor"), None, None, None),
        P(("shard", "tensor"), None, None, None),
        P(),
        P(),
        P(),
        P(),
    )
    out_specs = (
        P(None, ("shard", "tensor"), None),
        P(None, ("shard", "tensor"), None),
        P(None, ("shard", "tensor"), None),
        P(("shard", "tensor"), None, None, None),
        P(("shard", "tensor"), None, None, None),
        P(),
        P(),
        P(),
    )
    return jax.shard_map(
        per_device, mesh=mesh, in_specs=in_specs, out_specs=out_specs, check_vma=False
    )
```

```python
import jax
import jax.numpy as jnp
from jax import lax
from jax.sharding import PartitionSpec as P

BLOCK = 128


PRECISE = lax.Precision.HIGHEST


def adam_moments(grad_wide, mean_old, square_old):
    mean_new = 0.9 * mean_old + 0.1 * grad_wide
    square_new = 0.95 * square_old + 0.05 * grad_wide * grad_wide
    return (mean_new, square_new, mean_new / (jnp.sqrt(square_new) + 1e-08))


def per_device(
    gradients,
    adam_mean,
    adam_square,
    stat_left,
    stat_right,
    root_left,
    root_right,
    owners,
    small_grad,
    small_mean,
    small_square,
):
    layer_count, row_count, col_count = gradients.shape
    block_count = col_count // BLOCK
    devices = lax.axis_size(("shard", "tensor"))
    slot_count = stat_left.shape[1]
    total_blocks = owners.shape[0]
    positions = jnp.arange(total_blocks, dtype=jnp.int32)
    earlier = (owners[:, None] == owners[None, :]) & (positions[None, :] < positions[:, None])
    slot_index = jnp.sum(earlier.astype(jnp.int32), axis=1)
    target = slot_index * devices + owners
    places = jnp.arange(slot_count * devices, dtype=jnp.int32)
    picker = (
        (places[:, None] == target[None, :])
        .astype(jnp.bfloat16)
        .reshape(slot_count * devices, layer_count, block_count)
    )
    grad_wide = gradients.astype(jnp.float32)
    mean_out, square_out, direction = adam_moments(grad_wide, adam_mean, adam_square)
    adam_part = jnp.sum(
        jnp.square(direction).reshape(layer_count, row_count, block_count, BLOCK), axis=(1, 3)
    )
    part_by_place = jnp.zeros((slot_count * devices,), jnp.float32).at[target].set(
        adam_part.reshape(total_blocks)
    )
    part_hi = part_by_place.astype(jnp.bfloat16)
    part_lo = (part_by_place - part_hi.astype(jnp.float32)).astype(jnp.bfloat16)
    lane = jnp.arange(BLOCK, dtype=jnp.int32)
    extra = jnp.where(
        lane[None, :] == 0,
        part_hi[:, None],
        jnp.where(lane[None, :] == 1, part_lo[:, None], jnp.zeros((), jnp.bfloat16)),
    )[:, None, :]
    pieces = gradients.reshape(layer_count, row_count, block_count, BLOCK)
    outgoing = jnp.einsum(
        "qln,lrnb->qrb", picker, pieces, preferred_element_type=jnp.float32
    ).astype(jnp.bfloat16)
    outgoing = jnp.concatenate([outgoing, extra], axis=1)
    outgoing = outgoing.reshape(slot_count, devices, row_count + 1, BLOCK)
    incoming = lax.all_to_all(
        outgoing, ("shard", "tensor"), split_axis=1, concat_axis=1, tiled=True
    )
    block_grads = incoming[:, :, :row_count, :].reshape(slot_count, devices * row_count, BLOCK)
    adam_sums = jnp.sum(
        incoming[:, :, row_count, 0].astype(jnp.float32)
        + incoming[:, :, row_count, 1].astype(jnp.float32),
        axis=1,
    )
    left_out = (
        stat_left
        + jnp.einsum("cib,cjb->cij", block_grads, block_grads, preferred_element_type=jnp.float32)[
            None
        ]
    )
    right_out = (
        stat_right
        + jnp.einsum("cib,cid->cbd", block_grads, block_grads, preferred_element_type=jnp.float32)[
            None
        ]
    )
    left_applied = jnp.einsum(
        "cij,cjb->cib", root_left[0], block_grads.astype(jnp.float32), precision=PRECISE
    )
    precond = jnp.einsum("cib,cbd->cid", left_applied, root_right[0], precision=PRECISE)
    precond_sums = jnp.sum(jnp.square(precond), axis=(1, 2))
    graft_ratio = jnp.sqrt(adam_sums / (precond_sums + 1e-06))
    scaled = precond * graft_ratio[:, None, None]
    shaped = scaled.reshape(slot_count, devices, row_count, BLOCK)
    returned = lax.all_to_all(shaped, ("shard", "tensor"), split_axis=1, concat_axis=1, tiled=True)
    slot_ids = jnp.arange(slot_count, dtype=jnp.int32)
    device_ids = jnp.arange(devices, dtype=jnp.int32)
    placer = (
        (slot_index[:, None, None] == slot_ids[None, :, None])
        & (owners[:, None, None] == device_ids[None, None, :])
    ).astype(jnp.float32).reshape(layer_count, block_count, slot_count, devices)
    updates = jnp.einsum(
        "lnqd,qdrb->lrnb", placer, returned, precision=PRECISE,
        preferred_element_type=jnp.float32,
    ).reshape(layer_count, row_count, col_count)
    small_mean_out, small_square_out, small_update = adam_moments(
        small_grad, small_mean, small_square
    )
    return (
        updates,
        mean_out,
        square_out,
        left_out,
        right_out,
        small_update,
        small_mean_out,
        small_square_out,
    )


def solution(mesh):
    in_specs = (
        P(None, ("shard", "tensor"), None),
        P(None, ("shard", "tensor"), None),
        P(None, ("shard", "tensor"), None),
        P(("shard", "tensor"), None, None, None),
        P(("shard", "tensor"), None, None, None),
        P(("shard", "tensor"), None, None, None),
        P(("shard", "tensor"), None, None, None),
        P(),
        P(),
        P(),
        P(),
    )
    out_specs = (
        P(None, ("shard", "tensor"), None),
        P(None, ("shard", "tensor"), None),
        P(None, ("shard", "tensor"), None),
        P(("shard", "tensor"), None, None, None),
        P(("shard", "tensor"), None, None, None),
        P(),
        P(),
        P(),
    )
    return jax.shard_map(
        per_device, mesh=mesh, in_specs=in_specs, out_specs=out_specs, check_vma=False
    )
```

```python
import jax
import jax.numpy as jnp
from jax import lax
from jax.sharding import PartitionSpec as P

BLOCK = 128


PRECISE = lax.Precision.HIGHEST


def adam_moments(grad_wide, mean_old, square_old):
    mean_new = 0.9 * mean_old + 0.1 * grad_wide
    square_new = 0.95 * square_old + 0.05 * grad_wide * grad_wide
    return (mean_new, square_new, mean_new / (jnp.sqrt(square_new) + 1e-08))


def per_device(
    gradients,
    adam_mean,
    adam_square,
    stat_left,
    stat_right,
    root_left,
    root_right,
    owners,
    small_grad,
    small_mean,
    small_square,
):
    layer_count, row_count, col_count = gradients.shape
    block_count = col_count // BLOCK
    devices = lax.axis_size(("shard", "tensor"))
    slot_count = stat_left.shape[1]
    total_blocks = owners.shape[0]
    positions = jnp.arange(total_blocks, dtype=jnp.int32)
    earlier = (owners[:, None] == owners[None, :]) & (positions[None, :] < positions[:, None])
    slot_index = jnp.sum(earlier.astype(jnp.int32), axis=1)
    target = slot_index * devices + owners
    places = jnp.arange(slot_count * devices, dtype=jnp.int32)
    picker = (
        (places[:, None] == target[None, :])
        .astype(jnp.bfloat16)
        .reshape(slot_count * devices, layer_count, block_count)
    )
    grad_wide = gradients.astype(jnp.float32)
    mean_out, square_out, direction = adam_moments(grad_wide, adam_mean, adam_square)
    adam_part = jnp.sum(
        jnp.square(direction).reshape(layer_count, row_count, block_count, BLOCK), axis=(1, 3)
    )
    block_hi = adam_part.astype(jnp.bfloat16)
    block_lo = (adam_part - block_hi.astype(jnp.float32)).astype(jnp.bfloat16)
    halves = jnp.einsum(
        "qln,lnk->qk", picker, jnp.stack([block_hi, block_lo], axis=-1),
        preferred_element_type=jnp.float32,
    ).astype(jnp.bfloat16)
    part_hi = halves[:, 0]
    part_lo = halves[:, 1]
    lane = jnp.arange(BLOCK, dtype=jnp.int32)
    extra = jnp.where(
        lane[None, :] == 0,
        part_hi[:, None],
        jnp.where(lane[None, :] == 1, part_lo[:, None], jnp.zeros((), jnp.bfloat16)),
    )[:, None, :]
    pieces = gradients.reshape(layer_count, row_count, block_count, BLOCK)
    outgoing = jnp.einsum(
        "qln,lrnb->qrb", picker, pieces, preferred_element_type=jnp.float32
    ).astype(jnp.bfloat16)
    outgoing = jnp.concatenate([outgoing, extra], axis=1)
    outgoing = outgoing.reshape(slot_count, devices, row_count + 1, BLOCK)
    incoming = lax.all_to_all(
        outgoing, ("shard", "tensor"), split_axis=1, concat_axis=1, tiled=True
    )
    block_grads = incoming[:, :, :row_count, :].reshape(slot_count, devices * row_count, BLOCK)
    adam_sums = jnp.sum(
        incoming[:, :, row_count, 0].astype(jnp.float32)
        + incoming[:, :, row_count, 1].astype(jnp.float32),
        axis=1,
    )
    left_out = (
        stat_left
        + jnp.einsum("cib,cjb->cij", block_grads, block_grads, preferred_element_type=jnp.float32)[
            None
        ]
    )
    right_out = (
        stat_right
        + jnp.einsum("cib,cid->cbd", block_grads, block_grads, preferred_element_type=jnp.float32)[
            None
        ]
    )
    left_applied = jnp.einsum(
        "cij,cjb->cib", root_left[0], block_grads.astype(jnp.float32), precision=PRECISE
    )
    precond = jnp.einsum("cib,cbd->cid", left_applied, root_right[0], precision=PRECISE)
    precond_sums = jnp.sum(jnp.square(precond), axis=(1, 2))
    graft_ratio = jnp.sqrt(adam_sums / (precond_sums + 1e-06))
    scaled = precond * graft_ratio[:, None, None]
    shaped = scaled.reshape(slot_count, devices, row_count, BLOCK)
    returned = lax.all_to_all(shaped, ("shard", "tensor"), split_axis=1, concat_axis=1, tiled=True)
    slot_ids = jnp.arange(slot_count, dtype=jnp.int32)
    device_ids = jnp.arange(devices, dtype=jnp.int32)
    placer = (
        (slot_index[:, None, None] == slot_ids[None, :, None])
        & (owners[:, None, None] == device_ids[None, None, :])
    ).astype(jnp.float32).reshape(layer_count, block_count, slot_count, devices)
    updates = jnp.einsum(
        "lnqd,qdrb->lrnb", placer, returned, precision=PRECISE,
        preferred_element_type=jnp.float32,
    ).reshape(layer_count, row_count, col_count)
    small_mean_out, small_square_out, small_update = adam_moments(
        small_grad, small_mean, small_square
    )
    return (
        updates,
        mean_out,
        square_out,
        left_out,
        right_out,
        small_update,
        small_mean_out,
        small_square_out,
    )


def solution(mesh):
    in_specs = (
        P(None, ("shard", "tensor"), None),
        P(None, ("shard", "tensor"), None),
        P(None, ("shard", "tensor"), None),
        P(("shard", "tensor"), None, None, None),
        P(("shard", "tensor"), None, None, None),
        P(("shard", "tensor"), None, None, None),
        P(("shard", "tensor"), None, None, None),
        P(),
        P(),
        P(),
        P(),
    )
    out_specs = (
        P(None, ("shard", "tensor"), None),
        P(None, ("shard", "tensor"), None),
        P(None, ("shard", "tensor"), None),
        P(("shard", "tensor"), None, None, None),
        P(("shard", "tensor"), None, None, None),
        P(),
        P(),
        P(),
    )
    return jax.shard_map(
        per_device, mesh=mesh, in_specs=in_specs, out_specs=out_specs, check_vma=False
    )
```

```python
import jax
import jax.numpy as jnp
from jax import lax
from jax.sharding import PartitionSpec as P

BLOCK = 128


PRECISE = lax.Precision.HIGHEST


def adam_moments(grad_wide, mean_old, square_old):
    mean_new = 0.9 * mean_old + 0.1 * grad_wide
    square_new = 0.95 * square_old + 0.05 * grad_wide * grad_wide
    return (mean_new, square_new, mean_new / (jnp.sqrt(square_new) + 1e-08))


def per_device(
    gradients,
    adam_mean,
    adam_square,
    stat_left,
    stat_right,
    root_left,
    root_right,
    owners,
    small_grad,
    small_mean,
    small_square,
):
    layer_count, row_count, col_count = gradients.shape
    block_count = col_count // BLOCK
    devices = lax.axis_size(("shard", "tensor"))
    slot_count = stat_left.shape[1]
    total_blocks = owners.shape[0]
    positions = jnp.arange(total_blocks, dtype=jnp.int32)
    earlier = (owners[:, None] == owners[None, :]) & (positions[None, :] < positions[:, None])
    slot_index = jnp.sum(earlier.astype(jnp.int32), axis=1)
    target = slot_index * devices + owners
    places = jnp.arange(slot_count * devices, dtype=jnp.int32)
    picker = (
        (places[:, None] == target[None, :])
        .astype(jnp.bfloat16)
        .reshape(slot_count * devices, layer_count, block_count)
    )
    grad_wide = gradients.astype(jnp.float32)
    mean_out, square_out, direction = adam_moments(grad_wide, adam_mean, adam_square)
    adam_part = jnp.sum(
        jnp.square(direction).reshape(layer_count, row_count, block_count, BLOCK), axis=(1, 3)
    )
    block_hi = adam_part.astype(jnp.bfloat16)
    block_lo = (adam_part - block_hi.astype(jnp.float32)).astype(jnp.bfloat16)
    halves = jnp.einsum(
        "qln,lnk->qk", picker, jnp.stack([block_hi, block_lo], axis=-1),
        preferred_element_type=jnp.float32,
    ).astype(jnp.bfloat16)
    part_hi = halves[:, 0]
    part_lo = halves[:, 1]
    lane = jnp.arange(BLOCK, dtype=jnp.int32)
    extra = jnp.where(
        lane[None, :] == 0,
        part_hi[:, None],
        jnp.where(lane[None, :] == 1, part_lo[:, None], jnp.zeros((), jnp.bfloat16)),
    )[:, None, :]
    pieces = gradients.reshape(layer_count, row_count, block_count, BLOCK)
    outgoing = jnp.einsum(
        "qln,lrnb->qrb", picker, pieces, preferred_element_type=jnp.float32
    ).astype(jnp.bfloat16)
    outgoing = jnp.concatenate([outgoing, extra], axis=1)
    outgoing = outgoing.reshape(slot_count, devices, row_count + 1, BLOCK)
    incoming = lax.all_to_all(
        outgoing, ("shard", "tensor"), split_axis=1, concat_axis=1, tiled=True
    )
    block_grads = incoming[:, :, :row_count, :].reshape(slot_count, devices * row_count, BLOCK)
    adam_sums = jnp.sum(
        incoming[:, :, row_count, 0].astype(jnp.float32)
        + incoming[:, :, row_count, 1].astype(jnp.float32),
        axis=1,
    )
    left_out = (
        stat_left
        + jnp.einsum("cib,cjb->cij", block_grads, block_grads, preferred_element_type=jnp.float32)[
            None
        ]
    )
    right_out = (
        stat_right
        + jnp.einsum("cib,cid->cbd", block_grads, block_grads, preferred_element_type=jnp.float32)[
            None
        ]
    )
    left_applied = jnp.einsum(
        "cij,cjb->cib", root_left[0], block_grads.astype(jnp.float32), precision=PRECISE
    )
    precond = jnp.einsum("cib,cbd->cid", left_applied, root_right[0], precision=PRECISE)
    precond_sums = jnp.sum(jnp.square(precond), axis=(1, 2))
    graft_ratio = jnp.sqrt(adam_sums / (precond_sums + 1e-06))
    scaled = precond * graft_ratio[:, None, None]
    shaped = scaled.reshape(slot_count, devices, row_count, BLOCK)
    returned = lax.all_to_all(shaped, ("shard", "tensor"), split_axis=1, concat_axis=1, tiled=True)
    slot_ids = jnp.arange(slot_count, dtype=jnp.int32)
    device_ids = jnp.arange(devices, dtype=jnp.int32)
    placer = (
        (slot_index[:, None, None] == slot_ids[None, :, None])
        & (owners[:, None, None] == device_ids[None, None, :])
    ).astype(jnp.float32).reshape(layer_count, block_count, slot_count, devices)
    updates = (
        jnp.einsum(
            "lnqd,qdrb->lnrb", placer, returned, precision=PRECISE,
            preferred_element_type=jnp.float32,
        )
        .transpose(0, 2, 1, 3)
        .reshape(layer_count, row_count, col_count)
    )
    small_mean_out, small_square_out, small_update = adam_moments(
        small_grad, small_mean, small_square
    )
    return (
        updates,
        mean_out,
        square_out,
        left_out,
        right_out,
        small_update,
        small_mean_out,
        small_square_out,
    )


def solution(mesh):
    in_specs = (
        P(None, ("shard", "tensor"), None),
        P(None, ("shard", "tensor"), None),
        P(None, ("shard", "tensor"), None),
        P(("shard", "tensor"), None, None, None),
        P(("shard", "tensor"), None, None, None),
        P(("shard", "tensor"), None, None, None),
        P(("shard", "tensor"), None, None, None),
        P(),
        P(),
        P(),
        P(),
    )
    out_specs = (
        P(None, ("shard", "tensor"), None),
        P(None, ("shard", "tensor"), None),
        P(None, ("shard", "tensor"), None),
        P(("shard", "tensor"), None, None, None),
        P(("shard", "tensor"), None, None, None),
        P(),
        P(),
        P(),
    )
    return jax.shard_map(
        per_device, mesh=mesh, in_specs=in_specs, out_specs=out_specs, check_vma=False
    )
```

```python
import jax
import jax.numpy as jnp
from jax import lax
from jax.sharding import PartitionSpec as P

BLOCK = 128


PRECISE = lax.Precision.HIGHEST


def adam_moments(grad_wide, mean_old, square_old):
    mean_new = 0.9 * mean_old + 0.1 * grad_wide
    square_new = 0.95 * square_old + 0.05 * grad_wide * grad_wide
    return (mean_new, square_new, mean_new / (jnp.sqrt(square_new) + 1e-08))


def per_device(
    gradients,
    adam_mean,
    adam_square,
    stat_left,
    stat_right,
    root_left,
    root_right,
    owners,
    small_grad,
    small_mean,
    small_square,
):
    layer_count, row_count, col_count = gradients.shape
    block_count = col_count // BLOCK
    devices = lax.axis_size(("shard", "tensor"))
    slot_count = stat_left.shape[1]
    total_blocks = owners.shape[0]
    positions = jnp.arange(total_blocks, dtype=jnp.int32)
    earlier = (owners[:, None] == owners[None, :]) & (positions[None, :] < positions[:, None])
    slot_index = jnp.sum(earlier.astype(jnp.int32), axis=1)
    target = slot_index * devices + owners
    places = jnp.arange(slot_count * devices, dtype=jnp.int32)
    picker = (
        (places[:, None] == target[None, :])
        .astype(jnp.bfloat16)
        .reshape(slot_count * devices, layer_count, block_count)
    )
    grad_wide = gradients.astype(jnp.float32)
    mean_out, square_out, direction = adam_moments(grad_wide, adam_mean, adam_square)
    adam_part = jnp.sum(
        jnp.square(direction).reshape(layer_count, row_count, block_count, BLOCK), axis=(1, 3)
    )
    block_hi = adam_part.astype(jnp.bfloat16)
    block_lo = (adam_part - block_hi.astype(jnp.float32)).astype(jnp.bfloat16)
    halves = jnp.einsum(
        "qln,lnk->qk", picker, jnp.stack([block_hi, block_lo], axis=-1),
        preferred_element_type=jnp.float32,
    ).astype(jnp.bfloat16)
    part_slot = jnp.pad(
        halves.reshape(slot_count, devices, 2).transpose(1, 2, 0),
        ((0, 0), (0, row_count - 2), (0, BLOCK - slot_count)),
    )[None]
    pieces = gradients.reshape(layer_count, row_count, block_count, BLOCK)
    outgoing = jnp.einsum(
        "qln,lrnb->qrb", picker, pieces, preferred_element_type=jnp.float32
    ).astype(jnp.bfloat16)
    outgoing = jnp.concatenate(
        [outgoing.reshape(slot_count, devices, row_count, BLOCK), part_slot], axis=0
    )
    incoming = lax.all_to_all(
        outgoing, ("shard", "tensor"), split_axis=1, concat_axis=1, tiled=True
    )
    block_grads = incoming[:slot_count].reshape(slot_count, devices * row_count, BLOCK)
    adam_sums = jnp.sum(
        incoming[slot_count, :, 0:2, 0:slot_count].astype(jnp.float32), axis=(0, 1)
    )
    left_out = (
        stat_left
        + jnp.einsum("cib,cjb->cij", block_grads, block_grads, preferred_element_type=jnp.float32)[
            None
        ]
    )
    right_out = (
        stat_right
        + jnp.einsum("cib,cid->cbd", block_grads, block_grads, preferred_element_type=jnp.float32)[
            None
        ]
    )
    left_applied = jnp.einsum(
        "cij,cjb->cib", root_left[0], block_grads.astype(jnp.float32), precision=PRECISE
    )
    precond = jnp.einsum("cib,cbd->cid", left_applied, root_right[0], precision=PRECISE)
    precond_sums = jnp.sum(jnp.square(precond), axis=(1, 2))
    graft_ratio = jnp.sqrt(adam_sums / (precond_sums + 1e-06))
    scaled = precond * graft_ratio[:, None, None]
    shaped = scaled.reshape(slot_count, devices, row_count, BLOCK)
    returned = lax.all_to_all(shaped, ("shard", "tensor"), split_axis=1, concat_axis=1, tiled=True)
    slot_ids = jnp.arange(slot_count, dtype=jnp.int32)
    device_ids = jnp.arange(devices, dtype=jnp.int32)
    placer = (
        (slot_index[:, None, None] == slot_ids[None, :, None])
        & (owners[:, None, None] == device_ids[None, None, :])
    ).astype(jnp.float32).reshape(layer_count, block_count, slot_count, devices)
    updates = (
        jnp.einsum(
            "lnqd,qdrb->lnrb", placer, returned, precision=PRECISE,
            preferred_element_type=jnp.float32,
        )
        .transpose(0, 2, 1, 3)
        .reshape(layer_count, row_count, col_count)
    )
    small_mean_out, small_square_out, small_update = adam_moments(
        small_grad, small_mean, small_square
    )
    return (
        updates,
        mean_out,
        square_out,
        left_out,
        right_out,
        small_update,
        small_mean_out,
        small_square_out,
    )


def solution(mesh):
    in_specs = (
        P(None, ("shard", "tensor"), None),
        P(None, ("shard", "tensor"), None),
        P(None, ("shard", "tensor"), None),
        P(("shard", "tensor"), None, None, None),
        P(("shard", "tensor"), None, None, None),
        P(("shard", "tensor"), None, None, None),
        P(("shard", "tensor"), None, None, None),
        P(),
        P(),
        P(),
        P(),
    )
    out_specs = (
        P(None, ("shard", "tensor"), None),
        P(None, ("shard", "tensor"), None),
        P(None, ("shard", "tensor"), None),
        P(("shard", "tensor"), None, None, None),
        P(("shard", "tensor"), None, None, None),
        P(),
        P(),
        P(),
    )
    return jax.shard_map(
        per_device, mesh=mesh, in_specs=in_specs, out_specs=out_specs, check_vma=False
    )
```

```python
import jax
import jax.numpy as jnp
from jax import lax
from jax.sharding import PartitionSpec as P

BLOCK = 128


PRECISE = lax.Precision.HIGHEST


def adam_moments(grad_wide, mean_old, square_old):
    mean_new = 0.9 * mean_old + 0.1 * grad_wide
    square_new = 0.95 * square_old + 0.05 * grad_wide * grad_wide
    return (mean_new, square_new, mean_new / (jnp.sqrt(square_new) + 1e-08))


def per_device(
    gradients,
    adam_mean,
    adam_square,
    stat_left,
    stat_right,
    root_left,
    root_right,
    owners,
    small_grad,
    small_mean,
    small_square,
):
    layer_count, row_count, col_count = gradients.shape
    block_count = col_count // BLOCK
    devices = lax.axis_size(("shard", "tensor"))
    slot_count = stat_left.shape[1]
    total_blocks = owners.shape[0]
    positions = jnp.arange(total_blocks, dtype=jnp.int32)
    earlier = (owners[:, None] == owners[None, :]) & (positions[None, :] < positions[:, None])
    slot_index = jnp.sum(earlier.astype(jnp.int32), axis=1)
    target = slot_index * devices + owners
    places = jnp.arange(slot_count * devices, dtype=jnp.int32)
    picker = (
        (places[:, None] == target[None, :])
        .astype(jnp.bfloat16)
        .reshape(slot_count * devices, layer_count, block_count)
    )
    grad_wide = gradients.astype(jnp.float32)
    _, _, direction = adam_moments(grad_wide, adam_mean, adam_square)
    mean_out, square_out, _ = adam_moments(
        *lax.optimization_barrier((grad_wide, adam_mean, adam_square))
    )
    adam_part = jnp.sum(
        jnp.square(direction).reshape(layer_count, row_count, block_count, BLOCK), axis=(1, 3)
    )
    block_hi = adam_part.astype(jnp.bfloat16)
    block_lo = (adam_part - block_hi.astype(jnp.float32)).astype(jnp.bfloat16)
    halves = jnp.einsum(
        "qln,lnk->qk", picker, jnp.stack([block_hi, block_lo], axis=-1),
        preferred_element_type=jnp.float32,
    ).astype(jnp.bfloat16)
    part_hi = halves[:, 0]
    part_lo = halves[:, 1]
    lane = jnp.arange(BLOCK, dtype=jnp.int32)
    extra = jnp.where(
        lane[None, :] == 0,
        part_hi[:, None],
        jnp.where(lane[None, :] == 1, part_lo[:, None], jnp.zeros((), jnp.bfloat16)),
    )[:, None, :]
    pieces = gradients.reshape(layer_count, row_count, block_count, BLOCK)
    outgoing = jnp.einsum(
        "qln,lrnb->qrb", picker, pieces, preferred_element_type=jnp.float32
    ).astype(jnp.bfloat16)
    outgoing = jnp.concatenate([outgoing, extra], axis=1)
    outgoing = outgoing.reshape(slot_count, devices, row_count + 1, BLOCK)
    incoming = lax.all_to_all(
        outgoing, ("shard", "tensor"), split_axis=1, concat_axis=1, tiled=True
    )
    block_grads = incoming[:, :, :row_count, :].reshape(slot_count, devices * row_count, BLOCK)
    adam_sums = jnp.sum(
        incoming[:, :, row_count, 0].astype(jnp.float32)
        + incoming[:, :, row_count, 1].astype(jnp.float32),
        axis=1,
    )
    left_out = (
        stat_left
        + jnp.einsum("cib,cjb->cij", block_grads, block_grads, preferred_element_type=jnp.float32)[
            None
        ]
    )
    right_out = (
        stat_right
        + jnp.einsum("cib,cid->cbd", block_grads, block_grads, preferred_element_type=jnp.float32)[
            None
        ]
    )
    left_applied = jnp.einsum(
        "cij,cjb->cib", root_left[0], block_grads.astype(jnp.float32), precision=PRECISE
    )
    precond = jnp.einsum("cib,cbd->cid", left_applied, root_right[0], precision=PRECISE)
    precond_sums = jnp.sum(jnp.square(precond), axis=(1, 2))
    graft_ratio = jnp.sqrt(adam_sums / (precond_sums + 1e-06))
    scaled = precond * graft_ratio[:, None, None]
    shaped = scaled.reshape(slot_count, devices, row_count, BLOCK)
    returned = lax.all_to_all(shaped, ("shard", "tensor"), split_axis=1, concat_axis=1, tiled=True)
    slot_ids = jnp.arange(slot_count, dtype=jnp.int32)
    device_ids = jnp.arange(devices, dtype=jnp.int32)
    placer = (
        (slot_index[:, None, None] == slot_ids[None, :, None])
        & (owners[:, None, None] == device_ids[None, None, :])
    ).astype(jnp.float32).reshape(layer_count, block_count, slot_count, devices)
    updates = (
        jnp.einsum(
            "lnqd,qdrb->lnrb", placer, returned, precision=PRECISE,
            preferred_element_type=jnp.float32,
        )
        .transpose(0, 2, 1, 3)
        .reshape(layer_count, row_count, col_count)
    )
    small_mean_out, small_square_out, small_update = adam_moments(
        small_grad, small_mean, small_square
    )
    return (
        updates,
        mean_out,
        square_out,
        left_out,
        right_out,
        small_update,
        small_mean_out,
        small_square_out,
    )


def solution(mesh):
    in_specs = (
        P(None, ("shard", "tensor"), None),
        P(None, ("shard", "tensor"), None),
        P(None, ("shard", "tensor"), None),
        P(("shard", "tensor"), None, None, None),
        P(("shard", "tensor"), None, None, None),
        P(("shard", "tensor"), None, None, None),
        P(("shard", "tensor"), None, None, None),
        P(),
        P(),
        P(),
        P(),
    )
    out_specs = (
        P(None, ("shard", "tensor"), None),
        P(None, ("shard", "tensor"), None),
        P(None, ("shard", "tensor"), None),
        P(("shard", "tensor"), None, None, None),
        P(("shard", "tensor"), None, None, None),
        P(),
        P(),
        P(),
    )
    return jax.shard_map(
        per_device, mesh=mesh, in_specs=in_specs, out_specs=out_specs, check_vma=False
    )
```

```python
import jax
import jax.numpy as jnp
from jax import lax
from jax.sharding import PartitionSpec as P

BLOCK = 128


PRECISE = lax.Precision.HIGHEST
NEAR = lax.Precision.HIGH


def adam_moments(grad_wide, mean_old, square_old):
    mean_new = 0.9 * mean_old + 0.1 * grad_wide
    square_new = 0.95 * square_old + 0.05 * grad_wide * grad_wide
    return (mean_new, square_new, mean_new / (jnp.sqrt(square_new) + 1e-08))


def per_device(
    gradients,
    adam_mean,
    adam_square,
    stat_left,
    stat_right,
    root_left,
    root_right,
    owners,
    small_grad,
    small_mean,
    small_square,
):
    layer_count, row_count, col_count = gradients.shape
    block_count = col_count // BLOCK
    devices = lax.axis_size(("shard", "tensor"))
    slot_count = stat_left.shape[1]
    total_blocks = owners.shape[0]
    positions = jnp.arange(total_blocks, dtype=jnp.int32)
    earlier = (owners[:, None] == owners[None, :]) & (positions[None, :] < positions[:, None])
    slot_index = jnp.sum(earlier.astype(jnp.int32), axis=1)
    target = slot_index * devices + owners
    places = jnp.arange(slot_count * devices, dtype=jnp.int32)
    picker = (
        (places[:, None] == target[None, :])
        .astype(jnp.bfloat16)
        .reshape(slot_count * devices, layer_count, block_count)
    )
    grad_wide = gradients.astype(jnp.float32)
    mean_out, square_out, direction = adam_moments(grad_wide, adam_mean, adam_square)
    adam_part = jnp.sum(
        jnp.square(direction).reshape(layer_count, row_count, block_count, BLOCK), axis=(1, 3)
    )
    block_hi = adam_part.astype(jnp.bfloat16)
    block_lo = (adam_part - block_hi.astype(jnp.float32)).astype(jnp.bfloat16)
    halves = jnp.einsum(
        "qln,lnk->qk", picker, jnp.stack([block_hi, block_lo], axis=-1),
        preferred_element_type=jnp.float32,
    ).astype(jnp.bfloat16)
    part_hi = halves[:, 0]
    part_lo = halves[:, 1]
    lane = jnp.arange(BLOCK, dtype=jnp.int32)
    extra = jnp.where(
        lane[None, :] == 0,
        part_hi[:, None],
        jnp.where(lane[None, :] == 1, part_lo[:, None], jnp.zeros((), jnp.bfloat16)),
    )[:, None, :]
    pieces = gradients.reshape(layer_count, row_count, block_count, BLOCK)
    outgoing = jnp.einsum(
        "qln,lrnb->qrb", picker, pieces, preferred_element_type=jnp.float32
    ).astype(jnp.bfloat16)
    outgoing = jnp.concatenate([outgoing, extra], axis=1)
    outgoing = outgoing.reshape(slot_count, devices, row_count + 1, BLOCK)
    incoming = lax.all_to_all(
        outgoing, ("shard", "tensor"), split_axis=1, concat_axis=1, tiled=True
    )
    block_grads = incoming[:, :, :row_count, :].reshape(slot_count, devices * row_count, BLOCK)
    adam_sums = jnp.sum(
        incoming[:, :, row_count, 0].astype(jnp.float32)
        + incoming[:, :, row_count, 1].astype(jnp.float32),
        axis=1,
    )
    left_out = (
        stat_left
        + jnp.einsum("cib,cjb->cij", block_grads, block_grads, preferred_element_type=jnp.float32)[
            None
        ]
    )
    right_out = (
        stat_right
        + jnp.einsum("cib,cid->cbd", block_grads, block_grads, preferred_element_type=jnp.float32)[
            None
        ]
    )
    left_applied = jnp.einsum(
        "cij,cjb->cib", root_left[0], block_grads.astype(jnp.float32), precision=NEAR
    )
    precond = jnp.einsum("cib,cbd->cid", left_applied, root_right[0], precision=NEAR)
    precond_sums = jnp.sum(jnp.square(precond), axis=(1, 2))
    graft_ratio = jnp.sqrt(adam_sums / (precond_sums + 1e-06))
    scaled = precond * graft_ratio[:, None, None]
    shaped = scaled.reshape(slot_count, devices, row_count, BLOCK)
    returned = lax.all_to_all(shaped, ("shard", "tensor"), split_axis=1, concat_axis=1, tiled=True)
    slot_ids = jnp.arange(slot_count, dtype=jnp.int32)
    device_ids = jnp.arange(devices, dtype=jnp.int32)
    placer = (
        (slot_index[:, None, None] == slot_ids[None, :, None])
        & (owners[:, None, None] == device_ids[None, None, :])
    ).astype(jnp.float32).reshape(layer_count, block_count, slot_count, devices)
    updates = (
        jnp.einsum(
            "lnqd,qdrb->lnrb", placer, returned, precision=PRECISE,
            preferred_element_type=jnp.float32,
        )
        .transpose(0, 2, 1, 3)
        .reshape(layer_count, row_count, col_count)
    )
    small_mean_out, small_square_out, small_update = adam_moments(
        small_grad, small_mean, small_square
    )
    return (
        updates,
        mean_out,
        square_out,
        left_out,
        right_out,
        small_update,
        small_mean_out,
        small_square_out,
    )


def solution(mesh):
    in_specs = (
        P(None, ("shard", "tensor"), None),
        P(None, ("shard", "tensor"), None),
        P(None, ("shard", "tensor"), None),
        P(("shard", "tensor"), None, None, None),
        P(("shard", "tensor"), None, None, None),
        P(("shard", "tensor"), None, None, None),
        P(("shard", "tensor"), None, None, None),
        P(),
        P(),
        P(),
        P(),
    )
    out_specs = (
        P(None, ("shard", "tensor"), None),
        P(None, ("shard", "tensor"), None),
        P(None, ("shard", "tensor"), None),
        P(("shard", "tensor"), None, None, None),
        P(("shard", "tensor"), None, None, None),
        P(),
        P(),
        P(),
    )
    return jax.shard_map(
        per_device, mesh=mesh, in_specs=in_specs, out_specs=out_specs, check_vma=False
    )
```

```python
import jax
import jax.numpy as jnp
from jax import lax
from jax.sharding import PartitionSpec as P

BLOCK = 128


PRECISE = lax.Precision.HIGHEST
NEAR = lax.Precision.HIGH


def adam_moments(grad_wide, mean_old, square_old):
    mean_new = 0.9 * mean_old + 0.1 * grad_wide
    square_new = 0.95 * square_old + 0.05 * grad_wide * grad_wide
    return (mean_new, square_new, mean_new / (jnp.sqrt(square_new) + 1e-08))


def per_device(
    gradients,
    adam_mean,
    adam_square,
    stat_left,
    stat_right,
    root_left,
    root_right,
    owners,
    small_grad,
    small_mean,
    small_square,
):
    layer_count, row_count, col_count = gradients.shape
    block_count = col_count // BLOCK
    devices = lax.axis_size(("shard", "tensor"))
    slot_count = stat_left.shape[1]
    total_blocks = owners.shape[0]
    positions = jnp.arange(total_blocks, dtype=jnp.int32)
    earlier = (owners[:, None] == owners[None, :]) & (positions[None, :] < positions[:, None])
    slot_index = jnp.sum(earlier.astype(jnp.int32), axis=1)
    target = slot_index * devices + owners
    places = jnp.arange(slot_count * devices, dtype=jnp.int32)
    picker = (
        (places[:, None] == target[None, :])
        .astype(jnp.bfloat16)
        .reshape(slot_count * devices, layer_count, block_count)
    )
    grad_wide = gradients.astype(jnp.float32)
    mean_out, square_out, direction = adam_moments(grad_wide, adam_mean, adam_square)
    adam_part = jnp.sum(
        jnp.square(direction).reshape(layer_count, row_count, block_count, BLOCK), axis=(1, 3)
    )
    block_hi = adam_part.astype(jnp.bfloat16)
    block_lo = (adam_part - block_hi.astype(jnp.float32)).astype(jnp.bfloat16)
    halves = jnp.einsum(
        "qln,lnk->qk", picker, jnp.stack([block_hi, block_lo], axis=-1),
        preferred_element_type=jnp.float32,
    ).astype(jnp.bfloat16)
    part_hi = halves[:, 0]
    part_lo = halves[:, 1]
    lane = jnp.arange(BLOCK, dtype=jnp.int32)
    extra = jnp.where(
        lane[None, :] == 0,
        part_hi[:, None],
        jnp.where(lane[None, :] == 1, part_lo[:, None], jnp.zeros((), jnp.bfloat16)),
    )[:, None, :]
    pieces = gradients.reshape(layer_count, row_count, block_count, BLOCK)
    outgoing = jnp.einsum(
        "qln,lrnb->qrb", picker, pieces, preferred_element_type=jnp.float32
    ).astype(jnp.bfloat16)
    outgoing = jnp.concatenate([outgoing, extra], axis=1)
    outgoing = outgoing.reshape(slot_count, devices, row_count + 1, BLOCK)
    incoming = lax.all_to_all(
        outgoing, ("shard", "tensor"), split_axis=1, concat_axis=1, tiled=True
    )
    block_grads = incoming[:, :, :row_count, :].reshape(slot_count, devices * row_count, BLOCK)
    adam_sums = jnp.sum(
        incoming[:, :, row_count, 0].astype(jnp.float32)
        + incoming[:, :, row_count, 1].astype(jnp.float32),
        axis=1,
    )
    left_out = (
        stat_left
        + jnp.einsum("cib,cjb->cij", block_grads, block_grads, preferred_element_type=jnp.float32)[
            None
        ]
    )
    right_out = (
        stat_right
        + jnp.einsum("cib,cid->cbd", block_grads, block_grads, preferred_element_type=jnp.float32)[
            None
        ]
    )
    left_applied = jnp.einsum(
        "cij,cjb->cib", root_left[0], block_grads.astype(jnp.float32), precision=NEAR
    )
    precond = jnp.einsum("cib,cbd->cid", left_applied, root_right[0], precision=NEAR)
    precond_sums = jnp.sum(jnp.square(precond), axis=(1, 2))
    graft_ratio = jnp.sqrt(adam_sums / (precond_sums + 1e-06))
    scaled = precond * graft_ratio[:, None, None]
    shaped = scaled.reshape(slot_count, devices, row_count, BLOCK)
    returned = lax.all_to_all(shaped, ("shard", "tensor"), split_axis=1, concat_axis=1, tiled=True)
    slot_ids = jnp.arange(slot_count, dtype=jnp.int32)
    device_ids = jnp.arange(devices, dtype=jnp.int32)
    placer = (
        (slot_index[:, None, None] == slot_ids[None, :, None])
        & (owners[:, None, None] == device_ids[None, None, :])
    ).astype(jnp.float32).reshape(layer_count, block_count, slot_count, devices)
    updates = (
        jnp.einsum(
            "lnqd,qdrb->lnrb", placer, returned, precision=NEAR,
            preferred_element_type=jnp.float32,
        )
        .transpose(0, 2, 1, 3)
        .reshape(layer_count, row_count, col_count)
    )
    small_mean_out, small_square_out, small_update = adam_moments(
        small_grad, small_mean, small_square
    )
    return (
        updates,
        mean_out,
        square_out,
        left_out,
        right_out,
        small_update,
        small_mean_out,
        small_square_out,
    )


def solution(mesh):
    in_specs = (
        P(None, ("shard", "tensor"), None),
        P(None, ("shard", "tensor"), None),
        P(None, ("shard", "tensor"), None),
        P(("shard", "tensor"), None, None, None),
        P(("shard", "tensor"), None, None, None),
        P(("shard", "tensor"), None, None, None),
        P(("shard", "tensor"), None, None, None),
        P(),
        P(),
        P(),
        P(),
    )
    out_specs = (
        P(None, ("shard", "tensor"), None),
        P(None, ("shard", "tensor"), None),
        P(None, ("shard", "tensor"), None),
        P(("shard", "tensor"), None, None, None),
        P(("shard", "tensor"), None, None, None),
        P(),
        P(),
        P(),
    )
    return jax.shard_map(
        per_device, mesh=mesh, in_specs=in_specs, out_specs=out_specs, check_vma=False
    )
```

```python
import jax
import jax.numpy as jnp
from jax import lax
from jax.sharding import PartitionSpec as P

BLOCK = 128


PRECISE = lax.Precision.HIGHEST
NEAR = lax.Precision.HIGH


def adam_moments(grad_wide, mean_old, square_old):
    mean_new = 0.9 * mean_old + 0.1 * grad_wide
    square_new = 0.95 * square_old + 0.05 * grad_wide * grad_wide
    return (mean_new, square_new, mean_new / (jnp.sqrt(square_new) + 1e-08))


def per_device(
    gradients,
    adam_mean,
    adam_square,
    stat_left,
    stat_right,
    root_left,
    root_right,
    owners,
    small_grad,
    small_mean,
    small_square,
):
    layer_count, row_count, col_count = gradients.shape
    block_count = col_count // BLOCK
    devices = lax.axis_size(("shard", "tensor"))
    slot_count = stat_left.shape[1]
    total_blocks = owners.shape[0]
    positions = jnp.arange(total_blocks, dtype=jnp.int32)
    earlier = (owners[:, None] == owners[None, :]) & (positions[None, :] < positions[:, None])
    slot_index = jnp.dot(
        earlier.astype(jnp.bfloat16), jnp.ones((total_blocks,), jnp.bfloat16),
        preferred_element_type=jnp.float32,
    ).astype(jnp.int32)
    target = slot_index * devices + owners
    places = jnp.arange(slot_count * devices, dtype=jnp.int32)
    picker = (
        (places[:, None] == target[None, :])
        .astype(jnp.bfloat16)
        .reshape(slot_count * devices, layer_count, block_count)
    )
    grad_wide = gradients.astype(jnp.float32)
    mean_out, square_out, direction = adam_moments(grad_wide, adam_mean, adam_square)
    adam_part = jnp.sum(
        jnp.square(direction).reshape(layer_count, row_count, block_count, BLOCK), axis=(1, 3)
    )
    block_hi = adam_part.astype(jnp.bfloat16)
    block_lo = (adam_part - block_hi.astype(jnp.float32)).astype(jnp.bfloat16)
    halves = jnp.einsum(
        "qln,lnk->qk", picker, jnp.stack([block_hi, block_lo], axis=-1),
        preferred_element_type=jnp.float32,
    ).astype(jnp.bfloat16)
    part_hi = halves[:, 0]
    part_lo = halves[:, 1]
    lane = jnp.arange(BLOCK, dtype=jnp.int32)
    extra = jnp.where(
        lane[None, :] == 0,
        part_hi[:, None],
        jnp.where(lane[None, :] == 1, part_lo[:, None], jnp.zeros((), jnp.bfloat16)),
    )[:, None, :]
    pieces = gradients.reshape(layer_count, row_count, block_count, BLOCK)
    outgoing = jnp.einsum(
        "qln,lrnb->qrb", picker, pieces, preferred_element_type=jnp.float32
    ).astype(jnp.bfloat16)
    outgoing = jnp.concatenate([outgoing, extra], axis=1)
    outgoing = outgoing.reshape(slot_count, devices, row_count + 1, BLOCK)
    incoming = lax.all_to_all(
        outgoing, ("shard", "tensor"), split_axis=1, concat_axis=1, tiled=True
    )
    block_grads = incoming[:, :, :row_count, :].reshape(slot_count, devices * row_count, BLOCK)
    adam_sums = jnp.sum(
        incoming[:, :, row_count, 0].astype(jnp.float32)
        + incoming[:, :, row_count, 1].astype(jnp.float32),
        axis=1,
    )
    left_out = (
        stat_left
        + jnp.einsum("cib,cjb->cij", block_grads, block_grads, preferred_element_type=jnp.float32)[
            None
        ]
    )
    right_out = (
        stat_right
        + jnp.einsum("cib,cid->cbd", block_grads, block_grads, preferred_element_type=jnp.float32)[
            None
        ]
    )
    left_applied = jnp.einsum(
        "cij,cjb->cib", root_left[0], block_grads.astype(jnp.float32), precision=NEAR
    )
    precond = jnp.einsum("cib,cbd->cid", left_applied, root_right[0], precision=NEAR)
    precond_sums = jnp.sum(jnp.square(precond), axis=(1, 2))
    graft_ratio = jnp.sqrt(adam_sums / (precond_sums + 1e-06))
    scaled = precond * graft_ratio[:, None, None]
    shaped = scaled.reshape(slot_count, devices, row_count, BLOCK)
    returned = lax.all_to_all(shaped, ("shard", "tensor"), split_axis=1, concat_axis=1, tiled=True)
    slot_ids = jnp.arange(slot_count, dtype=jnp.int32)
    device_ids = jnp.arange(devices, dtype=jnp.int32)
    placer = (
        (slot_index[:, None, None] == slot_ids[None, :, None])
        & (owners[:, None, None] == device_ids[None, None, :])
    ).astype(jnp.float32).reshape(layer_count, block_count, slot_count, devices)
    updates = (
        jnp.einsum(
            "lnqd,qdrb->lnrb", placer, returned, precision=PRECISE,
            preferred_element_type=jnp.float32,
        )
        .transpose(0, 2, 1, 3)
        .reshape(layer_count, row_count, col_count)
    )
    small_mean_out, small_square_out, small_update = adam_moments(
        small_grad, small_mean, small_square
    )
    return (
        updates,
        mean_out,
        square_out,
        left_out,
        right_out,
        small_update,
        small_mean_out,
        small_square_out,
    )


def solution(mesh):
    in_specs = (
        P(None, ("shard", "tensor"), None),
        P(None, ("shard", "tensor"), None),
        P(None, ("shard", "tensor"), None),
        P(("shard", "tensor"), None, None, None),
        P(("shard", "tensor"), None, None, None),
        P(("shard", "tensor"), None, None, None),
        P(("shard", "tensor"), None, None, None),
        P(),
        P(),
        P(),
        P(),
    )
    out_specs = (
        P(None, ("shard", "tensor"), None),
        P(None, ("shard", "tensor"), None),
        P(None, ("shard", "tensor"), None),
        P(("shard", "tensor"), None, None, None),
        P(("shard", "tensor"), None, None, None),
        P(),
        P(),
        P(),
    )
    return jax.shard_map(
        per_device, mesh=mesh, in_specs=in_specs, out_specs=out_specs, check_vma=False
    )
```

```python
import jax
import jax.numpy as jnp
from jax import lax
from jax.sharding import PartitionSpec as P

BLOCK = 128


PRECISE = lax.Precision.HIGHEST
NEAR = lax.Precision.HIGH


def adam_moments(grad_wide, mean_old, square_old):
    mean_new = 0.9 * mean_old + 0.1 * grad_wide
    square_new = 0.95 * square_old + 0.05 * grad_wide * grad_wide
    return (mean_new, square_new, mean_new / (jnp.sqrt(square_new) + 1e-08))


def per_device(
    gradients,
    adam_mean,
    adam_square,
    stat_left,
    stat_right,
    root_left,
    root_right,
    owners,
    small_grad,
    small_mean,
    small_square,
):
    layer_count, row_count, col_count = gradients.shape
    block_count = col_count // BLOCK
    devices = lax.axis_size(("shard", "tensor"))
    slot_count = stat_left.shape[1]
    total_blocks = owners.shape[0]
    positions = jnp.arange(total_blocks, dtype=jnp.int32)
    earlier = (owners[:, None] == owners[None, :]) & (positions[None, :] < positions[:, None])
    slot_index = jnp.sum(earlier.astype(jnp.int32), axis=1)
    target = slot_index * devices + owners
    places = jnp.arange(slot_count * devices, dtype=jnp.int32)
    picker = (
        (places[:, None] == target[None, :])
        .astype(jnp.bfloat16)
        .reshape(slot_count * devices, layer_count, block_count)
    )
    grad_wide = gradients.astype(jnp.float32)
    mean_out, square_out, direction = adam_moments(grad_wide, adam_mean, adam_square)
    adam_part = jnp.sum(
        jnp.square(direction).reshape(layer_count, row_count, block_count, BLOCK), axis=(1, 3)
    )
    block_hi = adam_part.astype(jnp.bfloat16)
    block_lo = (adam_part - block_hi.astype(jnp.float32)).astype(jnp.bfloat16)
    halves = jnp.einsum(
        "qln,lnk->qk", picker, jnp.stack([block_hi, block_lo], axis=-1),
        preferred_element_type=jnp.float32,
    ).astype(jnp.bfloat16)
    part_hi = halves[:, 0]
    part_lo = halves[:, 1]
    lane = jnp.arange(BLOCK, dtype=jnp.int32)
    extra = jnp.where(
        lane[None, :] == 0,
        part_hi[:, None],
        jnp.where(lane[None, :] == 1, part_lo[:, None], jnp.zeros((), jnp.bfloat16)),
    )[:, None, :]
    pieces = gradients.reshape(layer_count, row_count, block_count, BLOCK)
    outgoing = jnp.einsum(
        "qln,lrnb->qrb", picker, pieces, preferred_element_type=jnp.float32
    ).astype(jnp.bfloat16)
    outgoing = jnp.concatenate([outgoing, extra], axis=1)
    outgoing = outgoing.reshape(slot_count, devices, row_count + 1, BLOCK)
    incoming = lax.all_to_all(
        outgoing, ("shard", "tensor"), split_axis=1, concat_axis=1, tiled=True
    )
    block_grads = incoming[:, :, :row_count, :].reshape(slot_count, devices * row_count, BLOCK)
    adam_sums = jnp.sum(incoming[:, :, row_count, 0:2].astype(jnp.float32), axis=(1, 2))
    left_out = (
        stat_left
        + jnp.einsum("cib,cjb->cij", block_grads, block_grads, preferred_element_type=jnp.float32)[
            None
        ]
    )
    right_out = (
        stat_right
        + jnp.einsum("cib,cid->cbd", block_grads, block_grads, preferred_element_type=jnp.float32)[
            None
        ]
    )
    left_applied = jnp.einsum(
        "cij,cjb->cib", root_left[0], block_grads.astype(jnp.float32), precision=NEAR
    )
    precond = jnp.einsum("cib,cbd->cid", left_applied, root_right[0], precision=NEAR)
    precond_sums = jnp.sum(jnp.square(precond), axis=(1, 2))
    graft_ratio = jnp.sqrt(adam_sums / (precond_sums + 1e-06))
    scaled = precond * graft_ratio[:, None, None]
    shaped = scaled.reshape(slot_count, devices, row_count, BLOCK)
    returned = lax.all_to_all(shaped, ("shard", "tensor"), split_axis=1, concat_axis=1, tiled=True)
    slot_ids = jnp.arange(slot_count, dtype=jnp.int32)
    device_ids = jnp.arange(devices, dtype=jnp.int32)
    placer = (
        (slot_index[:, None, None] == slot_ids[None, :, None])
        & (owners[:, None, None] == device_ids[None, None, :])
    ).astype(jnp.float32).reshape(layer_count, block_count, slot_count, devices)
    updates = (
        jnp.einsum(
            "lnqd,qdrb->lnrb", placer, returned, precision=PRECISE,
            preferred_element_type=jnp.float32,
        )
        .transpose(0, 2, 1, 3)
        .reshape(layer_count, row_count, col_count)
    )
    small_mean_out, small_square_out, small_update = adam_moments(
        small_grad, small_mean, small_square
    )
    return (
        updates,
        mean_out,
        square_out,
        left_out,
        right_out,
        small_update,
        small_mean_out,
        small_square_out,
    )


def solution(mesh):
    in_specs = (
        P(None, ("shard", "tensor"), None),
        P(None, ("shard", "tensor"), None),
        P(None, ("shard", "tensor"), None),
        P(("shard", "tensor"), None, None, None),
        P(("shard", "tensor"), None, None, None),
        P(("shard", "tensor"), None, None, None),
        P(("shard", "tensor"), None, None, None),
        P(),
        P(),
        P(),
        P(),
    )
    out_specs = (
        P(None, ("shard", "tensor"), None),
        P(None, ("shard", "tensor"), None),
        P(None, ("shard", "tensor"), None),
        P(("shard", "tensor"), None, None, None),
        P(("shard", "tensor"), None, None, None),
        P(),
        P(),
        P(),
    )
    return jax.shard_map(
        per_device, mesh=mesh, in_specs=in_specs, out_specs=out_specs, check_vma=False
    )
```
